256 devices in a mesh: sub: 16 (over y, z_lo, core), mem: 16 (over x, z_hi).
Axes of the slice: x: 4, y: 4, z: 8 (z_hi: 4, z_lo: 2; z = z_hi * 2 + z_lo), core: 2. Of those that a mesh axis runs over, the one named last changes fastest.
Arguments:
- now_field: float32 [128, 1024, 512], P('mem', 'sub'), may hold values from -6 to 6
- prev_field: float32 [128, 1024, 512], P('mem', 'sub'), may hold values from -6 to 6
- speed: float32 [1024, 512], P('sub'), may hold values from 0.05 to 0.45
- obs_cells: int32 [2048], P('sub'), may hold values from 0 to 32767
- obs_values: float32 [2048], replicated, may hold values from -6 to 6
- obs_precision: float32 [2048], replicated, may hold values from 0.1 to 1
- taper: float32 [2048, 2048], P(('sub', 'mem')), may hold values from 0.05 to 1
Outputs:
- now_analysis: float32 [128, 1024, 512], P('mem', 'sub')
- prev_analysis: float32 [128, 1024, 512], P('mem', 'sub')
The draws below stay inside these ranges and needn't reach their ends.
Inputs may be any that keep to these rules, and one draw needn't show every extreme that they name: `obs_cells`: entry o is a cell of subdomain o // 128, counted row by row within that subdomain's 64 x 512 cells.
All inputs are finite; a program needn't handle non-finite values.
Results may differ from the reference program's by a relative error of at most 0.00019.
Values sent between devices are 32-bit elements; how exact they have to be, the bound alone decides.
A program may use at most 64 MiB of HBM per device.

```python
import math
import jax
import jax.numpy as jnp
from jax import lax

ENS = 128
CX = 64
NY = 512
STEPS = 8
NS_ITERS = 8
BLOCK = 256
OBS = 2048
NX = 1024
NBLOCKS = 2048
OBS_SUB = 128


def place_ends(drawn, stream_key, least, high):
    longest = drawn.shape.index(max(drawn.shape))
    spots = []
    for shift in (0, 1):
        where = [jax.random.randint(jax.random.fold_in(stream_key, axis), (), 0, length) for axis, length in enumerate(drawn.shape)]
        where[longest] = (where[longest] + shift) % drawn.shape[longest]
        spots.append(tuple(where))
    return drawn.at[spots[0]].set(least).at[spots[1]].set(high)


def steps_of(own_key, shape, cuts, smallest, largest):
    gain, own = 1.0, jax.random.fold_in(own_key, 6)
    for dim, shards_of in cuts:
        heights = jnp.exp(jax.random.uniform(jax.random.fold_in(own, dim), (shards_of,), jnp.float32, smallest / len(cuts), largest / len(cuts)))
        gain = gain * jnp.repeat(heights, shape[dim] // shards_of).reshape([-1 if axis == dim else 1 for axis in range(len(shape))])
    return gain


def scatter_about(rng, extent, width, bound, cuts=(), kind=jnp.bfloat16):
    gain = steps_of(rng, extent, cuts, -0.22, 0.18) if cuts else 1.0
    array = jax.random.normal(rng, extent, jnp.float32) * width * gain
    return jnp.minimum(jnp.maximum(array, -bound), bound).astype(kind)


def setup_inputs(seed: int = 0) -> dict:
    keys = jax.random.split(jax.random.key(seed), 8)
    return {
        "now_field": scatter_about(keys[0], (ENS, NX, NY), 1.0, 6.0, ((0, 16), (1, 16)), jnp.float32),
        "prev_field": scatter_about(keys[1], (ENS, NX, NY), 1.0, 6.0, ((0, 16), (1, 16)), jnp.float32),
        "speed": jnp.clip(jnp.exp(math.log(0.45) - 2.1972245 * jax.random.uniform(keys[2], (NX, NY), jnp.float32) ** steps_of(keys[2], (NX, NY), ((0, 16),), -0.2, 0.2)), 0.05, 0.45),
        "obs_cells": place_ends(jax.random.randint(keys[3], (OBS,), 0, CX * NY), jax.random.fold_in(keys[3], 1), 0, (CX * NY) - 1).astype(jnp.int32),
        "obs_values": scatter_about(keys[4], (OBS,), 1.0, 6.0, (), jnp.float32),
        "obs_precision": jnp.clip(jnp.exp(jax.random.uniform(keys[5], (OBS,), jnp.float32, math.log(0.1), math.log(1.0))), 0.1, 1.0),
        "taper": jnp.clip(jnp.exp(math.log(1.0) - 2.9957323 * jax.random.uniform(keys[6], (NBLOCKS, OBS), jnp.float32) ** steps_of(keys[6], (NBLOCKS, OBS), ((0, 256),), -0.2, 0.2)), 0.05, 1.0),
    }


exact_mode = lax.Precision.HIGHEST

def leapfrog(current, previous, speed):
    padded = jnp.pad(current, ((0, 0), (1, 1), (1, 1)))
    spread = padded[:, 2:, 1:-1] + padded[:, :-2, 1:-1] + padded[:, 1:-1, 2:] + padded[:, 1:-1, :-2] - 4.0 * current
    return 2.0 * current - previous + speed * spread

def inverse_root(gram):
    eye = jnp.eye(gram.shape[-1], dtype=jnp.float32)
    scale = jnp.trace(gram, axis1=-2, axis2=-1)[..., None, None]
    iterate = gram / scale
    root = jnp.broadcast_to(eye, gram.shape)
    for sweep in range(NS_ITERS):
        factor = 1.5 * eye - 0.5 * jnp.matmul(root, iterate, precision=exact_mode)
        iterate = jnp.matmul(iterate, factor, precision=exact_mode)
        root = jnp.matmul(factor, root, precision=exact_mode)
    return root / jnp.sqrt(scale)

def reference(now_field, prev_field, speed, obs_cells, obs_values, obs_precision, taper):
    current, previous = (now_field, prev_field)
    for sweep in range(STEPS):
        current, previous = (leapfrog(current, previous, speed), current)
    flat_now = current.reshape(ENS, NX * NY)
    located = (jnp.arange(OBS, dtype=jnp.int32) // OBS_SUB * (CX * NY) + obs_cells).astype(jnp.int32)
    observed = jnp.take(flat_now, located, axis=1)
    obs_mean = lax.optimization_barrier(jnp.mean(observed, axis=0))
    obs_pert = observed - obs_mean
    misfit = obs_values - obs_mean
    stacked = jnp.stack((current, previous)).reshape(2, ENS, NBLOCKS, BLOCK)
    eye = jnp.eye(ENS, dtype=jnp.float32)

    def one_block(index):
        weight = taper[index] * obs_precision
        gram = (ENS - 1.0) * eye + jnp.dot(obs_pert * weight[None, :], obs_pert.T, precision=exact_mode)
        root_g = inverse_root(gram)
        pulled = jnp.dot(obs_pert, weight * misfit, precision=exact_mode)
        shift_w = jnp.dot(root_g, jnp.dot(root_g, pulled, precision=exact_mode), precision=exact_mode)
        mixing = math.sqrt(ENS - 1.0) * root_g + shift_w[:, None]
        block = lax.dynamic_index_in_dim(stacked, index, axis=2, keepdims=False)
        center = lax.optimization_barrier(jnp.mean(block, axis=1, keepdims=True))
        return center + jnp.einsum('jk,fjc->fkc', mixing, block - center, precision=exact_mode)
    result = lax.map(one_block, jnp.arange(NBLOCKS, dtype=jnp.int32))
    result = jnp.transpose(result, (1, 2, 0, 3)).reshape(2, ENS, NX, NY)
    return (result[0], result[1])
```

```python
import functools
import math

import jax
import jax.numpy as jnp
from jax import lax
from jax.experimental import pallas as pl
from jax.experimental.pallas import tpu as pltpu
from jax.sharding import PartitionSpec as P

ENS = 128
STEPS = 8
NS_ITERS = 8
BLOCK = 256
GROUP = 16
OWN = 8
ROWS = 64
STRIP = 4
COLS = 512
OBS_SUB = 128
TALL = ROWS + 2 * STEPS
MESH = pl.DeviceIdType.MESH
F32 = jnp.float32


def halves(x):
    high = x.astype(jnp.bfloat16)
    low = (x - high.astype(F32)).astype(jnp.bfloat16)
    return high, low


def side(x):
    return jnp.concatenate(halves(x), axis=1)


def tile(x):
    both = side(x)
    return jnp.concatenate([both, both], axis=0)


def product(left, right):
    wide = jnp.dot(left, right, preferred_element_type=F32)
    width = wide.shape[1] // 2
    return wide[:, :width] + wide[:, width:]


def forecast_rows(field, pace, step, low, high, unroll):
    source, target = (step + 1) % 2, step % 2
    lane = lax.broadcasted_iota(jnp.int32, (OWN, COLS), 1)

    def one(row, held):
        above, here = held
        below = field[source, row + 1]
        west = jnp.where(lane == 0, 0.0, pltpu.roll(here, 1, 1))
        east = jnp.where(lane == COLS - 1, 0.0, pltpu.roll(here, COLS - 1, 1))
        spread = below + above + east + west - 4.0 * here
        field[target, row] = 2.0 * here - field[target, row] + pace[row] * spread
        return here, below

    lax.fori_loop(low, high, one, (field[source, low - 1], field[source, low]), unroll=unroll)


def kernel(
    now_hbm,
    prev_hbm,
    speed_hbm,
    cells_ref,
    values_ref,
    precision_ref,
    taper_ref,
    now_out,
    prev_out,
    raw,
    rim,
    pace_raw,
    pace_rim,
    pace,
    field,
    seen,
    gram,
    iterate,
    root,
    arrived,
    leaving,
    settled,
    load_sem,
    rim_send,
    rim_recv,
    obs_send,
    obs_recv,
    out_send,
    out_recv,
    back_send,
    back_recv,
):
    mem, sub = lax.axis_index("mem"), lax.axis_index("sub")
    core = lax.rem(sub, 2)
    near = lax.rem(lax.div(sub, 2), 2)
    tier = lax.div(sub, 4)
    above = lax.rem(sub + GROUP - 1, GROUP)
    below = lax.rem(sub + 1, GROUP)
    twin = sub + 1 - 2 * core
    across = sub + 2 - 4 * near
    tiers = [lax.rem(sub + 4 * k, GROUP) for k in (1, 2, 3)]

    barrier = pltpu.get_barrier_semaphore()
    for other in (above, below, twin, across, *tiers):
        pl.semaphore_signal(barrier, inc=1, device_id={"sub": other}, device_id_type=MESH)

    def greet(step, _):
        pl.semaphore_signal(
            barrier, inc=1, device_id={"mem": lax.rem(mem + step, GROUP)}, device_id_type=MESH
        )
        return 0

    lax.fori_loop(1, GROUP, greet, 0)

    loads = [
        pltpu.make_async_copy(now_hbm, raw.at[0], load_sem.at[0]),
        pltpu.make_async_copy(prev_hbm, raw.at[1], load_sem.at[1]),
        pltpu.make_async_copy(speed_hbm, pace_raw, load_sem.at[2]),
    ]
    for load in loads:
        load.start()
    for load in loads:
        load.wait()

    pl.semaphore_wait(barrier, GROUP - 1 + 7)

    rims = []
    for side_index, (other, first) in enumerate(((below, ROWS - STEPS), (above, 0))):
        for index, source in enumerate((raw.at[0], raw.at[1])):
            rims.append(
                pltpu.make_async_remote_copy(
                    src_ref=source.at[:, first : first + STEPS, :],
                    dst_ref=rim.at[side_index, index],
                    send_sem=rim_send.at[side_index, index],
                    recv_sem=rim_recv.at[side_index, index],
                    device_id={"sub": other},
                    device_id_type=MESH,
                )
            )
        rims.append(
            pltpu.make_async_remote_copy(
                src_ref=pace_raw.at[first : first + STEPS, :],
                dst_ref=pace_rim.at[side_index],
                send_sem=rim_send.at[side_index, 2],
                recv_sem=rim_recv.at[side_index, 2],
                device_id={"sub": other},
                device_id_type=MESH,
            )
        )
    for copy in rims:
        copy.start()

    def turn(group, _):
        at = pl.multiple_of(group * 8, 8)
        for index in range(2):
            field[index, pl.ds(at + STEPS, 8)] = jnp.transpose(raw[index, :, pl.ds(at, 8), :], (1, 0, 2))
        rows = pace_raw[pl.ds(at, 8), :]
        pace[pl.ds(at + STEPS, 8)] = jnp.broadcast_to(rows[:, None, :], (8, OWN, COLS))
        return 0

    lax.fori_loop(0, ROWS // 8, turn, 0)

    for step in range(1, STEPS + 1):
        forecast_rows(field, pace, step, STEPS + step, STEPS + ROWS - step, 2)

    def ship(part, edges):
        def one(step, _):
            peer = lax.rem(mem + step, GROUP)
            outer = jnp.logical_or(peer < 2, peer > GROUP - 3)

            def go():
                pltpu.make_async_remote_copy(
                    src_ref=field.at[:, STEPS + STRIP * peer + part],
                    dst_ref=arrived.at[part, mem],
                    send_sem=out_send,
                    recv_sem=out_recv.at[part],
                    device_id={"mem": peer},
                    device_id_type=MESH,
                ).start()

            if edges is None:
                go()
            else:
                pl.when(outer if edges else jnp.logical_not(outer))(go)
            return 0

        lax.fori_loop(1, GROUP, one, 0)

    ship(0, False)

    for copy in rims:
        copy.wait_recv()
    for side_index, (at, outside) in enumerate(((0, sub == 0), (STEPS + ROWS, sub == GROUP - 1))):
        keep = jnp.where(outside, 0.0, 1.0)
        for index in range(2):
            field[index, at : at + STEPS] = jnp.transpose(rim[side_index, index], (1, 0, 2)) * keep
        rows = pace_rim[side_index] * keep
        pace[at : at + STEPS] = jnp.broadcast_to(rows[:, None, :], (STEPS, OWN, COLS))
    for step in range(1, STEPS + 1):
        forecast_rows(field, pace, step, step, STEPS + step, 2)
        forecast_rows(field, pace, step, STEPS + ROWS - step, ROWS + 2 * STEPS - step, 2)

    lane_all = lax.broadcasted_iota(jnp.int32, (OWN, COLS), 1)
    lane = lax.broadcasted_iota(jnp.int32, (OWN, OBS_SUB), 1)

    def pick(index, held):
        cell = cells_ref[index]
        row = field[0, STEPS + lax.div(cell, COLS)]
        kept = jnp.where(lane_all == lax.rem(cell, COLS), row, 0.0)
        kept = kept[:, :128] + kept[:, 128:256] + kept[:, 256:384] + kept[:, 384:]
        return jnp.where(lane == index, jnp.sum(kept, axis=1, keepdims=True), held)

    seen[core, tier, near, mem] = lax.fori_loop(
        0, OBS_SUB, pick, jnp.zeros((OWN, OBS_SUB), F32), unroll=8
    )

    def tell(step, _):
        pltpu.make_async_remote_copy(
            src_ref=seen.at[core, tier, near, mem],
            dst_ref=seen.at[core, tier, near, mem],
            send_sem=obs_send.at[0],
            recv_sem=obs_recv.at[0],
            device_id={"mem": lax.rem(mem + step, GROUP)},
            device_id_type=MESH,
        ).start()
        return 0

    lax.fori_loop(1, GROUP, tell, 0)

    ship(0, True)
    for part in range(1, STRIP):
        ship(part, None)
    for part in range(STRIP):
        arrived[part, mem] = field[:, STEPS + STRIP * mem + part]

    whole = seen.at[0, 0, 0, pl.ds(0, GROUP - 1)]
    pltpu.make_async_copy(whole, whole, obs_recv.at[0]).wait()

    def pass_on(block, other, number):
        copy = pltpu.make_async_remote_copy(
            src_ref=block,
            dst_ref=block,
            send_sem=obs_send.at[number],
            recv_sem=obs_recv.at[number],
            device_id={"sub": other},
            device_id_type=MESH,
        )
        copy.start()
        return copy

    own = seen.at[core, tier, near]
    met = seen.at[core, tier, 1 - near]
    crossing = pass_on(own, across, 1)
    for other in tiers:
        pass_on(own, other, 2)
    crossing.wait_recv()
    for other in tiers:
        pass_on(met, other, 3)
    third = seen.at[0, pl.ds(0, 3), 0]
    pltpu.make_async_copy(third, third, obs_recv.at[2]).wait()
    pltpu.make_async_copy(third, third, obs_recv.at[3]).wait()
    pass_on(seen.at[core], twin, 4).wait_recv()

    blocks = taper_ref.shape[0]
    lines = blocks * ENS
    gram[...] = jnp.zeros_like(gram)

    def gather_gram(index, _):
        lefts, rights = [], []
        for close in range(2):
            place = lax.rem(index, 4)
            sheet = lax.div(index, 4)
            observed = seen[sheet, place, close].reshape(ENS, OBS_SUB)
            mean = jnp.mean(observed, axis=0, keepdims=True)
            pert = observed - mean
            at = pl.ds(pl.multiple_of((4 * place + 2 * close + sheet) * OBS_SUB, OBS_SUB), OBS_SUB)
            weight = taper_ref[:, at] * precision_ref[:, at]
            pulling = weight * (values_ref[:, at] - mean)
            stack = [pert * weight[b : b + 1] for b in range(blocks)]
            lefts.append(side(jnp.concatenate([*stack, pulling, jnp.zeros_like(pulling)], axis=0)))
            high, low = halves(pert)
            rights.append(
                jnp.concatenate(
                    [jnp.concatenate([high, high], axis=1), jnp.concatenate([low, low], axis=1)], axis=0
                )
            )
        gram[...] += lax.dot_general(
            jnp.concatenate(lefts, axis=1),
            jnp.concatenate(rights, axis=1),
            (((1,), (1,)), ((), ())),
            preferred_element_type=F32,
        )
        return 0

    lax.fori_loop(0, GROUP // 2, gather_gram, 0)

    diagonal = lax.broadcasted_iota(jnp.int32, (ENS, ENS), 0) == lax.broadcasted_iota(
        jnp.int32, (ENS, ENS), 1
    )
    eye = jnp.where(diagonal, 1.0, 0.0)
    scales = []
    for b in range(blocks):
        wide = gram[b * ENS : (b + 1) * ENS, :]
        full = wide[:, :ENS] + wide[:, ENS:] + (ENS - 1.0) * eye
        scale = jnp.sum(jnp.sum(full * eye, axis=1, keepdims=True), axis=0, keepdims=True)
        scales.append(scale)
        iterate[b] = full / scale
        root[b] = eye

    def sweep(_, carry):
        for b in range(blocks):
            held, base = iterate[b], root[b]
            factor = 1.5 * eye - 0.5 * product(side(base), tile(held))
            iterate[b] = product(side(held), tile(factor))
            root[b] = product(side(factor), tile(base))
        return carry

    lax.fori_loop(0, NS_ITERS, sweep, 0)

    for b in range(blocks):
        final = root[b] / jnp.sqrt(scales[b])
        wide = gram[lines : lines + 8, :]
        pulled = (wide[:, :ENS] + wide[:, ENS:])[b : b + 1]
        pulled = jnp.broadcast_to(pulled, (16, ENS))
        right = tile(final)
        shift = product(side(product(side(pulled), right)), right)
        iterate[b] = math.sqrt(ENS - 1.0) * final + shift[0:1]

    def settle(part):
        for half in range(COLS // BLOCK):
            mixing = side(iterate[2 * part + half])
            cut = slice(half * BLOCK, (half + 1) * BLOCK)
            x = jnp.concatenate(
                [arrived[part, :, index, :, cut].reshape(ENS, BLOCK) for index in range(2)], axis=1
            )
            center = jnp.mean(x, axis=0, keepdims=True)
            moved = product(mixing, tile(x - center)) + center
            for index in range(2):
                leaving[part, :, index, :, cut] = moved[:, index * BLOCK : (index + 1) * BLOCK].reshape(
                    GROUP, OWN, BLOCK
                )

        def back(step, _):
            peer = lax.rem(mem + step, GROUP)
            pltpu.make_async_remote_copy(
                src_ref=leaving.at[part, peer],
                dst_ref=settled.at[:, STRIP * mem + part],
                send_sem=back_send,
                recv_sem=back_recv,
                device_id={"mem": peer},
                device_id_type=MESH,
            ).start()
            return 0

        lax.fori_loop(1, GROUP, back, 0)
        settled[:, STRIP * mem + part] = leaving[part, mem]

    for part in range(STRIP):
        strip = arrived.at[0, pl.ds(0, GROUP - 1)]
        pltpu.make_async_copy(strip, strip, out_recv.at[part]).wait()
        settle(part)

    everything = arrived.at[:, pl.ds(0, GROUP - 1)]
    pltpu.make_async_copy(everything, everything, back_recv).wait()

    def finish(group, _):
        at = pl.multiple_of(group * 8, 8)
        for index, out in enumerate((now_out, prev_out)):
            out[:, pl.ds(at, 8), :] = jnp.transpose(settled[index, pl.ds(at, 8)], (1, 0, 2))
        return 0

    lax.fori_loop(0, ROWS // 8, finish, 0)

    for copy in rims:
        copy.wait_send()
    pltpu.make_async_copy(whole, whole, obs_send.at[0]).wait()
    pltpu.make_async_copy(own, own, obs_send.at[1]).wait()
    pltpu.make_async_copy(third, third, obs_send.at[2]).wait()
    pltpu.make_async_copy(third, third, obs_send.at[3]).wait()
    pltpu.make_async_copy(seen.at[0], seen.at[0], obs_send.at[4]).wait()
    pltpu.make_async_copy(everything, everything, out_send).wait()
    pltpu.make_async_copy(everything, everything, back_send).wait()


def local(now_field, prev_field, speed, obs_cells, obs_values, obs_precision, taper):
    blocks = taper.shape[0]
    hbm = pl.BlockSpec(memory_space=pl.ANY)
    vmem = pl.BlockSpec(memory_space=pltpu.VMEM)
    outs = jax.ShapeDtypeStruct((OWN, ROWS, COLS), F32)
    return pl.pallas_call(
        kernel,
        out_shape=(outs, outs),
        in_specs=[hbm, hbm, hbm, pl.BlockSpec(memory_space=pltpu.SMEM), vmem, vmem, vmem],
        out_specs=(vmem, vmem),
        scratch_shapes=[
            pltpu.VMEM((2, OWN, ROWS, COLS), F32),
            pltpu.VMEM((2, 2, OWN, STEPS, COLS), F32),
            pltpu.VMEM((ROWS, COLS), F32),
            pltpu.VMEM((2, STEPS, COLS), F32),
            pltpu.VMEM((TALL, OWN, COLS), F32),
            pltpu.VMEM((2, TALL, OWN, COLS), F32),
            pltpu.VMEM((2, 4, 2, GROUP, OWN, OBS_SUB), F32),
            pltpu.VMEM((blocks * ENS + 16, 2 * ENS), F32),
            pltpu.VMEM((blocks, ENS, ENS), F32),
            pltpu.VMEM((blocks, ENS, ENS), F32),
            pltpu.VMEM((STRIP, GROUP, 2, OWN, COLS), F32),
            pltpu.VMEM((STRIP, GROUP, 2, OWN, COLS), F32),
            pltpu.VMEM((2, ROWS, OWN, COLS), F32),
            pltpu.SemaphoreType.DMA((3,)),
            pltpu.SemaphoreType.DMA((2, 3)),
            pltpu.SemaphoreType.DMA((2, 3)),
            pltpu.SemaphoreType.DMA((5,)),
            pltpu.SemaphoreType.DMA((5,)),
            pltpu.SemaphoreType.DMA,
            pltpu.SemaphoreType.DMA((STRIP,)),
            pltpu.SemaphoreType.DMA,
            pltpu.SemaphoreType.DMA,
        ],
        compiler_params=pltpu.CompilerParams(
            collective_id=0, has_side_effects=True, vmem_limit_bytes=48 * 2**20
        ),
    )(
        now_field,
        prev_field,
        speed,
        obs_cells,
        obs_values[None, :],
        obs_precision[None, :],
        taper,
    )


def solution(mesh):
    placed = (
        P("mem", "sub", None),
        P("mem", "sub", None),
        P("sub", None),
        P("sub"),
        P(),
        P(),
        P(("sub", "mem"), None),
    )
    return jax.shard_map(
        local,
        mesh=mesh,
        in_specs=placed,
        out_specs=(P("mem", "sub", None), P("mem", "sub", None)),
        check_vma=False,
    )
```

```python
import functools
import math

import jax
import jax.numpy as jnp
from jax import lax
from jax.experimental import pallas as pl
from jax.experimental.pallas import tpu as pltpu
from jax.sharding import PartitionSpec as P

ENS = 128
STEPS = 8
NS_ITERS = 8
BLOCK = 256
GROUP = 16
OWN = 8
ROWS = 64
STRIP = 4
COLS = 512
OBS_SUB = 128
TALL = ROWS + 2 * STEPS
AHEAD = 4
FIRST = 15
SHARES = (15, 20, 26, 30)
MESH = pl.DeviceIdType.MESH
F32 = jnp.float32


def halves(x):
    high = x.astype(jnp.bfloat16)
    low = (x - high.astype(F32)).astype(jnp.bfloat16)
    return high, low


def side(x):
    return jnp.concatenate(halves(x), axis=1)


def tile(x):
    both = side(x)
    return jnp.concatenate([both, both], axis=0)


def product(left, right):
    wide = jnp.dot(left, right, preferred_element_type=F32)
    width = wide.shape[1] // 2
    return wide[:, :width] + wide[:, width:]


def forecast_rows(field, pace, step, low, high):
    source, target = (step + 1) % 2, step % 2
    lane = lax.broadcasted_iota(jnp.int32, (high - low, OWN, COLS), 2)
    here = field[source, low:high]
    west = jnp.where(lane == 0, 0.0, pltpu.roll(here, 1, 2))
    east = jnp.where(lane == COLS - 1, 0.0, pltpu.roll(here, COLS - 1, 2))
    spread = field[source, low + 1 : high + 1] + field[source, low - 1 : high - 1] + east + west - 4.0 * here
    return 2.0 * here - field[target, low:high] + pace[low:high] * spread


def kernel(
    now_hbm,
    prev_hbm,
    speed_hbm,
    cells_ref,
    values_ref,
    precision_ref,
    taper_ref,
    now_out,
    prev_out,
    raw,
    rim,
    pace_raw,
    pace_rim,
    pace,
    field,
    seen,
    gram,
    iterate,
    root,
    arrived,
    leaving,
    settled,
    load_sem,
    rim_send,
    rim_recv,
    obs_send,
    obs_recv,
    out_send,
    out_recv,
    back_send,
    back_recv,
):
    mem, sub = lax.axis_index("mem"), lax.axis_index("sub")
    core = lax.rem(sub, 2)
    near = lax.rem(lax.div(sub, 2), 2)
    tier = lax.div(sub, 4)
    above = lax.rem(sub + GROUP - 1, GROUP)
    below = lax.rem(sub + 1, GROUP)
    twin = sub + 1 - 2 * core
    across = sub + 2 - 4 * near
    tiers = [lax.rem(sub + 4 * k, GROUP) for k in (1, 2, 3)]

    barrier = pltpu.get_barrier_semaphore()
    for other in (above, below, twin, across, *tiers):
        pl.semaphore_signal(barrier, inc=1, device_id={"sub": other}, device_id_type=MESH)

    def greet(step, _):
        pl.semaphore_signal(
            barrier, inc=1, device_id={"mem": lax.rem(mem + step, GROUP)}, device_id_type=MESH
        )
        return 0

    lax.fori_loop(1, GROUP, greet, 0)

    loads = [
        pltpu.make_async_copy(now_hbm, raw.at[0], load_sem.at[0]),
        pltpu.make_async_copy(prev_hbm, raw.at[1], load_sem.at[1]),
        pltpu.make_async_copy(speed_hbm, pace_raw, load_sem.at[2]),
    ]
    for load in loads:
        load.start()
    for load in loads:
        load.wait()

    def turn(group, _):
        at = pl.multiple_of(group * 8, 8)
        for index in range(2):
            field[index, pl.ds(at + STEPS, 8)] = jnp.transpose(raw[index, :, pl.ds(at, 8), :], (1, 0, 2))
        rows = pace_raw[pl.ds(at, 8), :]
        pace[pl.ds(at + STEPS, 8)] = jnp.broadcast_to(rows[:, None, :], (8, OWN, COLS))
        return 0

    lax.fori_loop(0, ROWS // 8, turn, 0)

    def inner(step):
        low, high = STEPS + step, STEPS + ROWS - step
        field[step % 2, low:high] = forecast_rows(field, pace, step, low, high)

    for step in range(1, AHEAD + 1):
        inner(step)

    pl.semaphore_wait(barrier, GROUP - 1 + 7)

    rims = []
    for side_index, (other, first) in enumerate(((below, ROWS - STEPS), (above, 0))):
        for index, source in enumerate((raw.at[0], raw.at[1])):
            rims.append(
                pltpu.make_async_remote_copy(
                    src_ref=source.at[:, first : first + STEPS, :],
                    dst_ref=rim.at[side_index, index],
                    send_sem=rim_send.at[side_index, index],
                    recv_sem=rim_recv.at[side_index, index],
                    device_id={"sub": other},
                    device_id_type=MESH,
                )
            )
        rims.append(
            pltpu.make_async_remote_copy(
                src_ref=pace_raw.at[first : first + STEPS, :],
                dst_ref=pace_rim.at[side_index],
                send_sem=rim_send.at[side_index, 2],
                recv_sem=rim_recv.at[side_index, 2],
                device_id={"sub": other},
                device_id_type=MESH,
            )
        )
    for copy in rims:
        copy.start()

    for step in range(AHEAD + 1, STEPS + 1):
        inner(step)


    def ship(first, last, early):
        def one(number, _):
            part = lax.div(number, GROUP - 1)
            step = lax.rem(number, GROUP - 1) + 1
            peer = lax.rem(mem + step, GROUP)
            ahead = jnp.logical_and(
                jnp.logical_and(peer >= 2, peer < GROUP - 2), jnp.logical_and(part == 0, step <= FIRST)
            )

            @pl.when(ahead if early else jnp.logical_not(ahead))
            def _():
                pltpu.make_async_remote_copy(
                    src_ref=field.at[:, STEPS + STRIP * peer + part],
                    dst_ref=arrived.at[part, mem],
                    send_sem=out_send,
                    recv_sem=out_recv.at[part],
                    device_id={"mem": peer},
                    device_id_type=MESH,
                ).start()

            return 0

        lax.fori_loop(first, last, one, 0)

    if FIRST:
        ship(0, FIRST, True)

    for copy in rims:
        copy.wait_recv()
    for side_index, (at, outside) in enumerate(((0, sub == 0), (STEPS + ROWS, sub == GROUP - 1))):
        keep = jnp.where(outside, 0.0, 1.0)
        for index in range(2):
            field[index, at : at + STEPS] = jnp.transpose(rim[side_index, index], (1, 0, 2)) * keep
        rows = pace_rim[side_index] * keep
        pace[at : at + STEPS] = jnp.broadcast_to(rows[:, None, :], (STEPS, OWN, COLS))
    for step in range(1, STEPS + 1):
        tops = step, STEPS + step
        ends = STEPS + ROWS - step, TALL - step
        upper = forecast_rows(field, pace, step, *tops)
        lower = forecast_rows(field, pace, step, *ends)
        field[step % 2, tops[0] : tops[1]] = upper
        field[step % 2, ends[0] : ends[1]] = lower

    lane_all = lax.broadcasted_iota(jnp.int32, (OWN, COLS), 1)
    lane = lax.broadcasted_iota(jnp.int32, (OWN, OBS_SUB), 1)

    def pick(index, held):
        cell = cells_ref[index]
        row = field[0, STEPS + lax.div(cell, COLS)]
        kept = jnp.where(lane_all == lax.rem(cell, COLS), row, 0.0)
        kept = kept[:, :128] + kept[:, 128:256] + kept[:, 256:384] + kept[:, 384:]
        return jnp.where(lane == index, jnp.sum(kept, axis=1, keepdims=True), held)

    seen[core, tier, near, mem] = lax.fori_loop(
        0, OBS_SUB, pick, jnp.zeros((OWN, OBS_SUB), F32), unroll=8
    )

    def tell(step, _):
        pltpu.make_async_remote_copy(
            src_ref=seen.at[core, tier, near, mem],
            dst_ref=seen.at[core, tier, near, mem],
            send_sem=obs_send.at[0],
            recv_sem=obs_recv.at[0],
            device_id={"mem": lax.rem(mem + step, GROUP)},
            device_id_type=MESH,
        ).start()
        return 0

    lax.fori_loop(1, GROUP, tell, 0)

    ship(0, SHARES[0], False)
    for part in range(STRIP):
        arrived[part, mem] = field[:, STEPS + STRIP * mem + part]

    whole = seen.at[0, 0, 0, pl.ds(0, GROUP - 1)]
    pltpu.make_async_copy(whole, whole, obs_recv.at[0]).wait()

    def pass_on(block, other, number):
        copy = pltpu.make_async_remote_copy(
            src_ref=block,
            dst_ref=block,
            send_sem=obs_send.at[number],
            recv_sem=obs_recv.at[number],
            device_id={"sub": other},
            device_id_type=MESH,
        )
        copy.start()
        return copy

    own = seen.at[core, tier, near]
    met = seen.at[core, tier, 1 - near]
    crossing = pass_on(own, across, 1)
    for other in tiers:
        pass_on(own, other, 2)
    ship(SHARES[0], SHARES[1], False)
    crossing.wait_recv()
    for other in tiers:
        pass_on(met, other, 3)
    ship(SHARES[1], SHARES[2], False)
    third = seen.at[0, pl.ds(0, 3), 0]
    pltpu.make_async_copy(third, third, obs_recv.at[2]).wait()
    pltpu.make_async_copy(third, third, obs_recv.at[3]).wait()
    swap = pass_on(seen.at[core], twin, 4)
    ship(SHARES[2], SHARES[3], False)
    swap.wait_recv()
    ship(SHARES[3], STRIP * (GROUP - 1), False)

    blocks = taper_ref.shape[0]
    lines = blocks * ENS
    gram[...] = jnp.zeros_like(gram)

    def gather_gram(index, _):
        lefts, rights = [], []
        for close in range(2):
            place = lax.rem(index, 4)
            sheet = lax.div(index, 4)
            observed = seen[sheet, place, close].reshape(ENS, OBS_SUB)
            mean = jnp.mean(observed, axis=0, keepdims=True)
            pert = observed - mean
            at = pl.ds(pl.multiple_of((4 * place + 2 * close + sheet) * OBS_SUB, OBS_SUB), OBS_SUB)
            weight = taper_ref[:, at] * precision_ref[:, at]
            pulling = weight * (values_ref[:, at] - mean)
            stack = [pert * weight[b : b + 1] for b in range(blocks)]
            lefts.append(side(jnp.concatenate([*stack, pulling, jnp.zeros_like(pulling)], axis=0)))
            high, low = halves(pert)
            rights.append(
                jnp.concatenate(
                    [jnp.concatenate([high, high], axis=1), jnp.concatenate([low, low], axis=1)], axis=0
                )
            )
        gram[...] += lax.dot_general(
            jnp.concatenate(lefts, axis=1),
            jnp.concatenate(rights, axis=1),
            (((1,), (1,)), ((), ())),
            preferred_element_type=F32,
        )
        return 0

    lax.fori_loop(0, GROUP // 2, gather_gram, 0)

    diagonal = lax.broadcasted_iota(jnp.int32, (ENS, ENS), 0) == lax.broadcasted_iota(
        jnp.int32, (ENS, ENS), 1
    )
    eye = jnp.where(diagonal, 1.0, 0.0)
    scales = []
    for b in range(blocks):
        wide = gram[b * ENS : (b + 1) * ENS, :]
        full = wide[:, :ENS] + wide[:, ENS:] + (ENS - 1.0) * eye
        scale = jnp.sum(jnp.sum(full * eye, axis=1, keepdims=True), axis=0, keepdims=True)
        scales.append(scale)
        iterate[b] = full / scale
        root[b] = eye

    def sweep(_, carry):
        for b in range(blocks):
            held, base = iterate[b], root[b]
            factor = 1.5 * eye - 0.5 * product(side(base), tile(held))
            iterate[b] = product(side(held), tile(factor))
            root[b] = product(side(factor), tile(base))
        return carry

    lax.fori_loop(0, NS_ITERS, sweep, 0)

    for b in range(blocks):
        final = root[b] / jnp.sqrt(scales[b])
        wide = gram[lines : lines + 8, :]
        pulled = (wide[:, :ENS] + wide[:, ENS:])[b : b + 1]
        pulled = jnp.broadcast_to(pulled, (16, ENS))
        right = tile(final)
        shift = product(side(product(side(pulled), right)), right)
        iterate[b] = math.sqrt(ENS - 1.0) * final + shift[0:1]

    def settle(part):
        for half in range(COLS // BLOCK):
            mixing = side(iterate[2 * part + half])
            cut = slice(half * BLOCK, (half + 1) * BLOCK)
            x = jnp.concatenate(
                [arrived[part, :, index, :, cut].reshape(ENS, BLOCK) for index in range(2)], axis=1
            )
            center = jnp.mean(x, axis=0, keepdims=True)
            moved = product(mixing, tile(x - center)) + center
            for index in range(2):
                leaving[part, :, index, :, cut] = moved[:, index * BLOCK : (index + 1) * BLOCK].reshape(
                    GROUP, OWN, BLOCK
                )

        def back(step, _):
            peer = lax.rem(mem + step, GROUP)
            pltpu.make_async_remote_copy(
                src_ref=leaving.at[part, peer],
                dst_ref=settled.at[:, STRIP * mem + part],
                send_sem=back_send,
                recv_sem=back_recv,
                device_id={"mem": peer},
                device_id_type=MESH,
            ).start()
            return 0

        lax.fori_loop(1, GROUP, back, 0)
        settled[:, STRIP * mem + part] = leaving[part, mem]

    for part in range(STRIP):
        strip = arrived.at[0, pl.ds(0, GROUP - 1)]
        pltpu.make_async_copy(strip, strip, out_recv.at[part]).wait()
        settle(part)

    everything = arrived.at[:, pl.ds(0, GROUP - 1)]
    pltpu.make_async_copy(everything, everything, back_recv).wait()

    def finish(group, _):
        at = pl.multiple_of(group * 8, 8)
        for index, out in enumerate((now_out, prev_out)):
            out[:, pl.ds(at, 8), :] = jnp.transpose(settled[index, pl.ds(at, 8)], (1, 0, 2))
        return 0

    lax.fori_loop(0, ROWS // 8, finish, 0)

    for copy in rims:
        copy.wait_send()
    pltpu.make_async_copy(whole, whole, obs_send.at[0]).wait()
    pltpu.make_async_copy(own, own, obs_send.at[1]).wait()
    pltpu.make_async_copy(third, third, obs_send.at[2]).wait()
    pltpu.make_async_copy(third, third, obs_send.at[3]).wait()
    pltpu.make_async_copy(seen.at[0], seen.at[0], obs_send.at[4]).wait()
    pltpu.make_async_copy(everything, everything, out_send).wait()
    pltpu.make_async_copy(everything, everything, back_send).wait()


def local(now_field, prev_field, speed, obs_cells, obs_values, obs_precision, taper):
    blocks = taper.shape[0]
    hbm = pl.BlockSpec(memory_space=pl.ANY)
    vmem = pl.BlockSpec(memory_space=pltpu.VMEM)
    outs = jax.ShapeDtypeStruct((OWN, ROWS, COLS), F32)
    return pl.pallas_call(
        kernel,
        out_shape=(outs, outs),
        in_specs=[hbm, hbm, hbm, pl.BlockSpec(memory_space=pltpu.SMEM), vmem, vmem, vmem],
        out_specs=(vmem, vmem),
        scratch_shapes=[
            pltpu.VMEM((2, OWN, ROWS, COLS), F32),
            pltpu.VMEM((2, 2, OWN, STEPS, COLS), F32),
            pltpu.VMEM((ROWS, COLS), F32),
            pltpu.VMEM((2, STEPS, COLS), F32),
            pltpu.VMEM((TALL, OWN, COLS), F32),
            pltpu.VMEM((2, TALL, OWN, COLS), F32),
            pltpu.VMEM((2, 4, 2, GROUP, OWN, OBS_SUB), F32),
            pltpu.VMEM((blocks * ENS + 16, 2 * ENS), F32),
            pltpu.VMEM((blocks, ENS, ENS), F32),
            pltpu.VMEM((blocks, ENS, ENS), F32),
            pltpu.VMEM((STRIP, GROUP, 2, OWN, COLS), F32),
            pltpu.VMEM((STRIP, GROUP, 2, OWN, COLS), F32),
            pltpu.VMEM((2, ROWS, OWN, COLS), F32),
            pltpu.SemaphoreType.DMA((3,)),
            pltpu.SemaphoreType.DMA((2, 3)),
            pltpu.SemaphoreType.DMA((2, 3)),
            pltpu.SemaphoreType.DMA((5,)),
            pltpu.SemaphoreType.DMA((5,)),
            pltpu.SemaphoreType.DMA,
            pltpu.SemaphoreType.DMA((STRIP,)),
            pltpu.SemaphoreType.DMA,
            pltpu.SemaphoreType.DMA,
        ],
        compiler_params=pltpu.CompilerParams(
            collective_id=0, has_side_effects=True, vmem_limit_bytes=60 * 2**20
        ),
    )(
        now_field,
        prev_field,
        speed,
        obs_cells,
        obs_values[None, :],
        obs_precision[None, :],
        taper,
    )


def solution(mesh):
    placed = (
        P("mem", "sub", None),
        P("mem", "sub", None),
        P("sub", None),
        P("sub"),
        P(),
        P(),
        P(("sub", "mem"), None),
    )
    return jax.shard_map(
        local,
        mesh=mesh,
        in_specs=placed,
        out_specs=(P("mem", "sub", None), P("mem", "sub", None)),
        check_vma=False,
    )
```

```python
import functools
import math

import jax
import jax.numpy as jnp
from jax import lax
from jax.experimental import pallas as pl
from jax.experimental.pallas import tpu as pltpu
from jax.sharding import PartitionSpec as P

ENS = 128
STEPS = 8
NS_ITERS = 8
BLOCK = 256
GROUP = 16
OWN = 8
ROWS = 64
STRIP = 4
COLS = 512
CHUNK = 16
OBS_SUB = 128
TALL = ROWS + 2 * STEPS
AHEAD = -1
MARGIN = 8
SHY = (STEPS + MARGIN) // STRIP
EARLY = 1
FIRST = 15
SHARES = (15, 20, 26, 30)
MESH = pl.DeviceIdType.MESH
F32 = jnp.float32


def halves(x):
    high = x.astype(jnp.bfloat16)
    low = (x - high.astype(F32)).astype(jnp.bfloat16)
    return high, low


def side(x):
    return jnp.concatenate(halves(x), axis=1)


def tile(x):
    both = side(x)
    return jnp.concatenate([both, both], axis=0)


def product(left, right):
    wide = jnp.dot(left, right, preferred_element_type=F32)
    width = wide.shape[1] // 2
    return wide[:, :width] + wide[:, width:]


def forecast_rows(field, pace, step, low, high):
    source, target = (step + 1) % 2, step % 2
    lane = lax.broadcasted_iota(jnp.int32, (high - low, OWN, COLS), 2)
    here = field[source, low:high]
    west = jnp.where(lane == 0, 0.0, pltpu.roll(here, 1, 2))
    east = jnp.where(lane == COLS - 1, 0.0, pltpu.roll(here, COLS - 1, 2))
    spread = field[source, low + 1 : high + 1] + field[source, low - 1 : high - 1] + east + west - 4.0 * here
    return 2.0 * here - field[target, low:high] + pace[low:high] * spread


def kernel(
    now_hbm,
    prev_hbm,
    speed_hbm,
    cells_ref,
    values_ref,
    precision_ref,
    taper_ref,
    settled,
    raw,
    rim,
    pace_raw,
    pace_rim,
    pace,
    field,
    seen,
    gram,
    iterate,
    root,
    arrived,
    leaving,
    load_sem,
    rim_send,
    rim_recv,
    obs_send,
    obs_recv,
    out_send,
    out_recv,
    back_send,
    back_recv,
    keep_sem,
):
    mem, sub = lax.axis_index("mem"), lax.axis_index("sub")
    core = lax.rem(sub, 2)
    near = lax.rem(lax.div(sub, 2), 2)
    tier = lax.div(sub, 4)
    above = lax.rem(sub + GROUP - 1, GROUP)
    below = lax.rem(sub + 1, GROUP)
    twin = sub + 1 - 2 * core
    across = sub + 2 - 4 * near
    tiers = [lax.rem(sub + 4 * k, GROUP) for k in (1, 2, 3)]

    barrier = pltpu.get_barrier_semaphore()
    for other in (above, below, twin, across, *tiers):
        pl.semaphore_signal(barrier, inc=1, device_id={"sub": other}, device_id_type=MESH)

    def greet(step, _):
        pl.semaphore_signal(
            barrier, inc=1, device_id={"mem": lax.rem(mem + step, GROUP)}, device_id_type=MESH
        )
        return 0

    lax.fori_loop(1, GROUP, greet, 0)

    def meet():
        pl.semaphore_wait(barrier, GROUP - 1 + 7)

        rims = []
        for side_index, (other, first) in enumerate(((below, ROWS - STEPS), (above, 0))):
            for index, source in enumerate((now_hbm, prev_hbm)):
                rims.append(
                    pltpu.make_async_remote_copy(
                        src_ref=source.at[:, first : first + STEPS, :],
                        dst_ref=rim.at[side_index, index],
                        send_sem=rim_send.at[side_index, index],
                        recv_sem=rim_recv.at[side_index, index],
                        device_id={"sub": other},
                        device_id_type=MESH,
                    )
                )
            rims.append(
                pltpu.make_async_remote_copy(
                    src_ref=speed_hbm.at[first : first + STEPS, :],
                    dst_ref=pace_rim.at[side_index],
                    send_sem=rim_send.at[side_index, 2],
                    recv_sem=rim_recv.at[side_index, 2],
                    device_id={"sub": other},
                    device_id_type=MESH,
                )
            )
        for copy in rims:
            copy.start()
        return rims

    loads = [
        pltpu.make_async_copy(now_hbm, raw.at[0], load_sem.at[0]),
        pltpu.make_async_copy(prev_hbm, raw.at[1], load_sem.at[1]),
        pltpu.make_async_copy(speed_hbm, pace_raw, load_sem.at[2]),
    ]
    for load in loads:
        load.start()
    if AHEAD < 0:
        rims = meet()
    for load in loads:
        load.wait()

    def turn(group, _):
        at = pl.multiple_of(group * 8, 8)
        for index in range(2):
            field[index, pl.ds(at + STEPS, 8)] = jnp.transpose(raw[index, :, pl.ds(at, 8), :], (1, 0, 2))
        rows = pace_raw[pl.ds(at, 8), :]
        pace[pl.ds(at + STEPS, 8)] = jnp.broadcast_to(rows[:, None, :], (8, OWN, COLS))
        return 0

    lax.fori_loop(0, ROWS // 8, turn, 0)

    def inner(step):
        low, high = STEPS + MARGIN + step, STEPS + ROWS - MARGIN - step
        field[step % 2, low:high] = forecast_rows(field, pace, step, low, high)

    for step in range(1, AHEAD + 1):
        inner(step)

    if AHEAD >= 0:
        rims = meet()
    for step in range(max(AHEAD, 0) + 1, STEPS + 1):
        inner(step)


    def ship(first, last, early):
        def one(number, _):
            part = lax.div(number, GROUP - 1)
            step = lax.rem(number, GROUP - 1) + 1
            peer = lax.rem(mem + step, GROUP)
            ahead = jnp.logical_and(
                jnp.logical_and(peer >= SHY, peer < GROUP - SHY), jnp.logical_and(part < EARLY, step <= FIRST)
            )

            @pl.when(ahead if early else jnp.logical_not(ahead))
            def _():
                pltpu.make_async_remote_copy(
                    src_ref=field.at[:, STEPS + STRIP * peer + part],
                    dst_ref=arrived.at[part, mem],
                    send_sem=out_send,
                    recv_sem=out_recv.at[part],
                    device_id={"mem": peer},
                    device_id_type=MESH,
                ).start()

            return 0

        lax.fori_loop(first, last, one, 0)

    if FIRST:
        ship(0, EARLY * (GROUP - 1), True)

    for copy in rims:
        copy.wait_recv()
    for side_index, (at, outside) in enumerate(((0, sub == 0), (STEPS + ROWS, sub == GROUP - 1))):
        keep = jnp.where(outside, 0.0, 1.0)
        for index in range(2):
            field[index, at : at + STEPS] = jnp.transpose(rim[side_index, index], (1, 0, 2)) * keep
        rows = pace_rim[side_index] * keep
        pace[at : at + STEPS] = jnp.broadcast_to(rows[:, None, :], (STEPS, OWN, COLS))
    for step in range(1, STEPS + 1):
        tops = step, STEPS + MARGIN + step
        ends = STEPS + ROWS - MARGIN - step, TALL - step
        upper = forecast_rows(field, pace, step, *tops)
        lower = forecast_rows(field, pace, step, *ends)
        field[step % 2, tops[0] : tops[1]] = upper
        field[step % 2, ends[0] : ends[1]] = lower

    lane_all = lax.broadcasted_iota(jnp.int32, (OWN, COLS), 1)
    lane = lax.broadcasted_iota(jnp.int32, (OWN, OBS_SUB), 1)

    def pick(index, held):
        cell = cells_ref[index]
        row = field[0, STEPS + lax.div(cell, COLS)]
        kept = jnp.where(lane_all == lax.rem(cell, COLS), row, 0.0)
        kept = kept[:, :128] + kept[:, 128:256] + kept[:, 256:384] + kept[:, 384:]
        return jnp.where(lane == index, jnp.sum(kept, axis=1, keepdims=True), held)

    seen[core, tier, near, mem] = lax.fori_loop(
        0, OBS_SUB, pick, jnp.zeros((OWN, OBS_SUB), F32), unroll=8
    )

    def tell(step, _):
        pltpu.make_async_remote_copy(
            src_ref=seen.at[core, tier, near, mem],
            dst_ref=seen.at[core, tier, near, mem],
            send_sem=obs_send.at[0],
            recv_sem=obs_recv.at[0],
            device_id={"mem": lax.rem(mem + step, GROUP)},
            device_id_type=MESH,
        ).start()
        return 0

    lax.fori_loop(1, GROUP, tell, 0)

    ship(0, SHARES[0], False)
    for part in range(STRIP):
        arrived[part, mem] = field[:, STEPS + STRIP * mem + part]

    whole = seen.at[0, 0, 0, pl.ds(0, GROUP - 1)]
    pltpu.make_async_copy(whole, whole, obs_recv.at[0]).wait()

    def pass_on(block, other, number):
        copy = pltpu.make_async_remote_copy(
            src_ref=block,
            dst_ref=block,
            send_sem=obs_send.at[number],
            recv_sem=obs_recv.at[number],
            device_id={"sub": other},
            device_id_type=MESH,
        )
        copy.start()
        return copy

    own = seen.at[core, tier, near]
    met = seen.at[core, tier, 1 - near]
    crossing = pass_on(own, across, 1)
    for other in tiers:
        pass_on(own, other, 2)
    ship(SHARES[0], SHARES[1], False)
    crossing.wait_recv()
    for other in tiers:
        pass_on(met, other, 3)
    ship(SHARES[1], SHARES[2], False)
    third = seen.at[0, pl.ds(0, 3), 0]
    pltpu.make_async_copy(third, third, obs_recv.at[2]).wait()
    pltpu.make_async_copy(third, third, obs_recv.at[3]).wait()
    swap = pass_on(seen.at[core], twin, 4)
    ship(SHARES[2], SHARES[3], False)
    swap.wait_recv()
    ship(SHARES[3], STRIP * (GROUP - 1), False)

    blocks = taper_ref.shape[0]
    lines = blocks * ENS
    gram[...] = jnp.zeros_like(gram)

    def gather_gram(index, _):
        lefts, rights = [], []
        for close in range(2):
            place = lax.rem(index, 4)
            sheet = lax.div(index, 4)
            observed = seen[sheet, place, close].reshape(ENS, OBS_SUB)
            mean = jnp.mean(observed, axis=0, keepdims=True)
            pert = observed - mean
            at = pl.ds(pl.multiple_of((4 * place + 2 * close + sheet) * OBS_SUB, OBS_SUB), OBS_SUB)
            weight = taper_ref[:, at] * precision_ref[:, at]
            pulling = weight * (values_ref[:, at] - mean)
            stack = [pert * weight[b : b + 1] for b in range(blocks)]
            lefts.append(side(jnp.concatenate([*stack, pulling, jnp.zeros_like(pulling)], axis=0)))
            high, low = halves(pert)
            rights.append(
                jnp.concatenate(
                    [jnp.concatenate([high, high], axis=1), jnp.concatenate([low, low], axis=1)], axis=0
                )
            )
        gram[...] += lax.dot_general(
            jnp.concatenate(lefts, axis=1),
            jnp.concatenate(rights, axis=1),
            (((1,), (1,)), ((), ())),
            preferred_element_type=F32,
        )
        return 0

    lax.fori_loop(0, GROUP // 2, gather_gram, 0)

    diagonal = lax.broadcasted_iota(jnp.int32, (ENS, ENS), 0) == lax.broadcasted_iota(
        jnp.int32, (ENS, ENS), 1
    )
    eye = jnp.where(diagonal, 1.0, 0.0)
    scales = []
    for b in range(blocks):
        wide = gram[b * ENS : (b + 1) * ENS, :]
        full = wide[:, :ENS] + wide[:, ENS:] + (ENS - 1.0) * eye
        scale = jnp.sum(jnp.sum(full * eye, axis=1, keepdims=True), axis=0, keepdims=True)
        scales.append(scale)
        iterate[b] = full / scale
        root[b] = eye

    def sweep(_, carry):
        for b in range(blocks):
            held, base = iterate[b], root[b]
            factor = 1.5 * eye - 0.5 * product(side(base), tile(held))
            iterate[b] = product(side(held), tile(factor))
            root[b] = product(side(factor), tile(base))
        return carry

    lax.fori_loop(0, NS_ITERS, sweep, 0)

    for b in range(blocks):
        final = root[b] / jnp.sqrt(scales[b])
        wide = gram[lines : lines + 8, :]
        pulled = (wide[:, :ENS] + wide[:, ENS:])[b : b + 1]
        pulled = jnp.broadcast_to(pulled, (16, ENS))
        right = tile(final)
        shift = product(side(product(side(pulled), right)), right)
        iterate[b] = math.sqrt(ENS - 1.0) * final + shift[0:1]

    def keep_own(part):
        return pltpu.make_async_copy(
            leaving.at[part, mem], settled.at[:, STRIP * mem + part], keep_sem.at[part]
        )

    def settle(part):
        for half in range(COLS // BLOCK):
            mixing = side(iterate[2 * part + half])
            cut = slice(half * BLOCK, (half + 1) * BLOCK)
            x = jnp.concatenate(
                [arrived[part, :, index, :, cut].reshape(ENS, BLOCK) for index in range(2)], axis=1
            )
            center = jnp.mean(x, axis=0, keepdims=True)
            moved = product(mixing, tile(x - center)) + center
            for index in range(2):
                leaving[part, :, index, :, cut] = moved[:, index * BLOCK : (index + 1) * BLOCK].reshape(
                    GROUP, OWN, BLOCK
                )

        def back(step, _):
            peer = lax.rem(mem + step, GROUP)
            pltpu.make_async_remote_copy(
                src_ref=leaving.at[part, peer],
                dst_ref=settled.at[:, STRIP * mem + part],
                send_sem=back_send,
                recv_sem=back_recv,
                device_id={"mem": peer},
                device_id_type=MESH,
            ).start()
            return 0

        lax.fori_loop(1, GROUP, back, 0)
        keep_own(part).start()

    for part in range(STRIP):
        strip = arrived.at[0, pl.ds(0, GROUP - 1)]
        pltpu.make_async_copy(strip, strip, out_recv.at[part]).wait()
        settle(part)

    everything = arrived.at[:, pl.ds(0, GROUP - 1)]
    pltpu.make_async_copy(everything, everything, back_recv).wait()

    for part in range(STRIP):
        keep_own(part).wait()
    for copy in rims:
        copy.wait_send()
    pltpu.make_async_copy(whole, whole, obs_send.at[0]).wait()
    pltpu.make_async_copy(own, own, obs_send.at[1]).wait()
    pltpu.make_async_copy(third, third, obs_send.at[2]).wait()
    pltpu.make_async_copy(third, third, obs_send.at[3]).wait()
    pltpu.make_async_copy(seen.at[0], seen.at[0], obs_send.at[4]).wait()
    pltpu.make_async_copy(everything, everything, out_send).wait()
    pltpu.make_async_copy(everything, everything, back_send).wait()


def turn_back(settled_hbm, now_hbm, prev_hbm, rows, turned, load_sem, store_sem):
    places = [(index, slice(at, at + CHUNK)) for index in range(2) for at in range(0, ROWS, CHUNK)]

    def load(number):
        index, at = places[number]
        return pltpu.make_async_copy(settled_hbm.at[index, at], rows.at[index, at], load_sem.at[number])

    def store(number):
        index, at = places[number]
        out = (now_hbm, prev_hbm)[index]
        return pltpu.make_async_copy(turned.at[index, :, at], out.at[:, at], store_sem.at[number])

    for number in range(len(places)):
        load(number).start()
    for number, (index, at) in enumerate(places):
        load(number).wait()
        turned[index, :, at] = jnp.transpose(rows[index, at], (1, 0, 2))
        store(number).start()
    for number in range(len(places)):
        store(number).wait()


def local(now_field, prev_field, speed, obs_cells, obs_values, obs_precision, taper):
    blocks = taper.shape[0]
    hbm = pl.BlockSpec(memory_space=pltpu.HBM)
    vmem = pl.BlockSpec(memory_space=pltpu.VMEM)
    outs = jax.ShapeDtypeStruct((OWN, ROWS, COLS), F32)
    settled = pl.pallas_call(
        kernel,
        out_shape=jax.ShapeDtypeStruct((2, ROWS, OWN, COLS), F32),
        in_specs=[hbm, hbm, hbm, pl.BlockSpec(memory_space=pltpu.SMEM), vmem, vmem, vmem],
        out_specs=hbm,
        scratch_shapes=[
            pltpu.VMEM((2, OWN, ROWS, COLS), F32),
            pltpu.VMEM((2, 2, OWN, STEPS, COLS), F32),
            pltpu.VMEM((ROWS, COLS), F32),
            pltpu.VMEM((2, STEPS, COLS), F32),
            pltpu.VMEM((TALL, OWN, COLS), F32),
            pltpu.VMEM((2, TALL, OWN, COLS), F32),
            pltpu.VMEM((2, 4, 2, GROUP, OWN, OBS_SUB), F32),
            pltpu.VMEM((blocks * ENS + 16, 2 * ENS), F32),
            pltpu.VMEM((blocks, ENS, ENS), F32),
            pltpu.VMEM((blocks, ENS, ENS), F32),
            pltpu.VMEM((STRIP, GROUP, 2, OWN, COLS), F32),
            pltpu.VMEM((STRIP, GROUP, 2, OWN, COLS), F32),
            pltpu.SemaphoreType.DMA((3,)),
            pltpu.SemaphoreType.DMA((2, 3)),
            pltpu.SemaphoreType.DMA((2, 3)),
            pltpu.SemaphoreType.DMA((5,)),
            pltpu.SemaphoreType.DMA((5,)),
            pltpu.SemaphoreType.DMA,
            pltpu.SemaphoreType.DMA((STRIP,)),
            pltpu.SemaphoreType.DMA,
            pltpu.SemaphoreType.DMA,
            pltpu.SemaphoreType.DMA((STRIP,)),
        ],
        compiler_params=pltpu.CompilerParams(
            collective_id=0, has_side_effects=True, vmem_limit_bytes=60 * 2**20
        ),
    )(
        now_field,
        prev_field,
        speed,
        obs_cells,
        obs_values[None, :],
        obs_precision[None, :],
        taper,
    )
    copies = 2 * ROWS // CHUNK
    return pl.pallas_call(
        turn_back,
        out_shape=(outs, outs),
        in_specs=[hbm],
        out_specs=(hbm, hbm),
        scratch_shapes=[
            pltpu.VMEM((2, ROWS, OWN, COLS), F32),
            pltpu.VMEM((2, OWN, ROWS, COLS), F32),
            pltpu.SemaphoreType.DMA((copies,)),
            pltpu.SemaphoreType.DMA((copies,)),
        ],
        compiler_params=pltpu.CompilerParams(vmem_limit_bytes=60 * 2**20),
    )(settled)


def solution(mesh):
    placed = (
        P("mem", "sub", None),
        P("mem", "sub", None),
        P("sub", None),
        P("sub"),
        P(),
        P(),
        P(("sub", "mem"), None),
    )
    return jax.shard_map(
        local,
        mesh=mesh,
        in_specs=placed,
        out_specs=(P("mem", "sub", None), P("mem", "sub", None)),
        check_vma=False,
    )
```

```python
import functools
import math

import jax
import jax.numpy as jnp
from jax import lax
from jax.experimental import pallas as pl
from jax.experimental.pallas import tpu as pltpu
from jax.sharding import PartitionSpec as P

ENS = 128
STEPS = 8
NS_ITERS = 8
BLOCK = 256
GROUP = 16
OWN = 8
ROWS = 64
STRIP = 4
COLS = 512
CHUNK = 16
OBS_SUB = 128
TALL = ROWS + 2 * STEPS
AHEAD = -1
MARGIN = 4
SHY = (STEPS + MARGIN) // STRIP
EARLY = 1
FIRST = 15
SHARES = (15, 24, 34, 44)
MESH = pl.DeviceIdType.MESH
F32 = jnp.float32


def halves(x):
    high = x.astype(jnp.bfloat16)
    low = (x - high.astype(F32)).astype(jnp.bfloat16)
    return high, low


def side(x):
    return jnp.concatenate(halves(x), axis=1)


def tile(x):
    both = side(x)
    return jnp.concatenate([both, both], axis=0)


def product(left, right):
    wide = jnp.dot(left, right, preferred_element_type=F32)
    width = wide.shape[1] // 2
    return wide[:, :width] + wide[:, width:]


def forecast_rows(field, pace, step, low, high):
    source, target = (step + 1) % 2, step % 2
    lane = lax.broadcasted_iota(jnp.int32, (high - low, OWN, COLS), 2)
    here = field[source, low:high]
    west = jnp.where(lane == 0, 0.0, pltpu.roll(here, 1, 2))
    east = jnp.where(lane == COLS - 1, 0.0, pltpu.roll(here, COLS - 1, 2))
    spread = field[source, low + 1 : high + 1] + field[source, low - 1 : high - 1] + east + west - 4.0 * here
    return 2.0 * here - field[target, low:high] + pace[low:high] * spread


def kernel(
    now_hbm,
    prev_hbm,
    speed_hbm,
    cells_ref,
    values_ref,
    precision_ref,
    taper_ref,
    settled,
    raw,
    rim,
    pace_raw,
    pace_rim,
    pace,
    field,
    seen,
    gram,
    iterate,
    root,
    arrived,
    leaving,
    load_sem,
    rim_send,
    rim_recv,
    obs_send,
    obs_recv,
    out_send,
    out_recv,
    back_send,
    back_recv,
    keep_sem,
):
    mem, sub = lax.axis_index("mem"), lax.axis_index("sub")
    core = lax.rem(sub, 2)
    near = lax.rem(lax.div(sub, 2), 2)
    tier = lax.div(sub, 4)
    above = lax.rem(sub + GROUP - 1, GROUP)
    below = lax.rem(sub + 1, GROUP)
    twin = sub + 1 - 2 * core
    across = sub + 2 - 4 * near
    tiers = [lax.rem(sub + 4 * k, GROUP) for k in (1, 2, 3)]

    barrier = pltpu.get_barrier_semaphore()
    for other in (above, below, twin, across, *tiers):
        pl.semaphore_signal(barrier, inc=1, device_id={"sub": other}, device_id_type=MESH)

    def greet(step, _):
        pl.semaphore_signal(
            barrier, inc=1, device_id={"mem": lax.rem(mem + step, GROUP)}, device_id_type=MESH
        )
        return 0

    lax.fori_loop(1, GROUP, greet, 0)

    def meet():
        pl.semaphore_wait(barrier, GROUP - 1 + 7)

        rims = []
        for side_index, (other, first) in enumerate(((below, ROWS - STEPS), (above, 0))):
            for index, source in enumerate((now_hbm, prev_hbm)):
                rims.append(
                    pltpu.make_async_remote_copy(
                        src_ref=source.at[:, first : first + STEPS, :],
                        dst_ref=rim.at[side_index, index],
                        send_sem=rim_send.at[side_index, index],
                        recv_sem=rim_recv.at[side_index, index],
                        device_id={"sub": other},
                        device_id_type=MESH,
                    )
                )
            rims.append(
                pltpu.make_async_remote_copy(
                    src_ref=speed_hbm.at[first : first + STEPS, :],
                    dst_ref=pace_rim.at[side_index],
                    send_sem=rim_send.at[side_index, 2],
                    recv_sem=rim_recv.at[side_index, 2],
                    device_id={"sub": other},
                    device_id_type=MESH,
                )
            )
        for copy in rims:
            copy.start()
        return rims

    loads = [
        pltpu.make_async_copy(now_hbm, raw.at[0], load_sem.at[0]),
        pltpu.make_async_copy(prev_hbm, raw.at[1], load_sem.at[1]),
        pltpu.make_async_copy(speed_hbm, pace_raw, load_sem.at[2]),
    ]
    for load in loads:
        load.start()
    if AHEAD < 0:
        rims = meet()
    for load in loads:
        load.wait()

    def turn(group, _):
        at = pl.multiple_of(group * 8, 8)
        for index in range(2):
            field[index, pl.ds(at + STEPS, 8)] = jnp.transpose(raw[index, :, pl.ds(at, 8), :], (1, 0, 2))
        rows = pace_raw[pl.ds(at, 8), :]
        pace[pl.ds(at + STEPS, 8)] = jnp.broadcast_to(rows[:, None, :], (8, OWN, COLS))
        return 0

    lax.fori_loop(0, ROWS // 8, turn, 0)

    def inner(step):
        low, high = STEPS + MARGIN + step, STEPS + ROWS - MARGIN - step
        field[step % 2, low:high] = forecast_rows(field, pace, step, low, high)

    for step in range(1, AHEAD + 1):
        inner(step)

    if AHEAD >= 0:
        rims = meet()
    for step in range(max(AHEAD, 0) + 1, STEPS + 1):
        inner(step)


    def ship(first, last, early):
        def one(number, _):
            part = lax.div(number, GROUP - 1)
            step = lax.rem(number, GROUP - 1) + 1
            peer = lax.rem(mem + step, GROUP)
            ahead = jnp.logical_and(
                jnp.logical_and(peer >= SHY, peer < GROUP - SHY), jnp.logical_and(part < EARLY, step <= FIRST)
            )

            @pl.when(ahead if early else jnp.logical_not(ahead))
            def _():
                pltpu.make_async_remote_copy(
                    src_ref=field.at[:, STEPS + STRIP * peer + part],
                    dst_ref=arrived.at[part, mem],
                    send_sem=out_send,
                    recv_sem=out_recv.at[part],
                    device_id={"mem": peer},
                    device_id_type=MESH,
                ).start()

            return 0

        lax.fori_loop(first, last, one, 0)

    if FIRST:
        ship(0, EARLY * (GROUP - 1), True)

    for copy in rims:
        copy.wait_recv()
    for side_index, (at, outside) in enumerate(((0, sub == 0), (STEPS + ROWS, sub == GROUP - 1))):
        keep = jnp.where(outside, 0.0, 1.0)
        for index in range(2):
            field[index, at : at + STEPS] = jnp.transpose(rim[side_index, index], (1, 0, 2)) * keep
        rows = pace_rim[side_index] * keep
        pace[at : at + STEPS] = jnp.broadcast_to(rows[:, None, :], (STEPS, OWN, COLS))
    for step in range(1, STEPS + 1):
        tops = step, STEPS + MARGIN + step
        ends = STEPS + ROWS - MARGIN - step, TALL - step
        upper = forecast_rows(field, pace, step, *tops)
        lower = forecast_rows(field, pace, step, *ends)
        field[step % 2, tops[0] : tops[1]] = upper
        field[step % 2, ends[0] : ends[1]] = lower

    lane_all = lax.broadcasted_iota(jnp.int32, (OWN, COLS), 1)
    lane = lax.broadcasted_iota(jnp.int32, (OWN, OBS_SUB), 1)

    def pick(index, held):
        cell = cells_ref[index]
        row = field[0, STEPS + lax.div(cell, COLS)]
        kept = jnp.where(lane_all == lax.rem(cell, COLS), row, 0.0)
        kept = kept[:, :128] + kept[:, 128:256] + kept[:, 256:384] + kept[:, 384:]
        return jnp.where(lane == index, jnp.sum(kept, axis=1, keepdims=True), held)

    seen[core, tier, near, mem] = lax.fori_loop(
        0, OBS_SUB, pick, jnp.zeros((OWN, OBS_SUB), F32), unroll=8
    )

    def tell(step, _):
        pltpu.make_async_remote_copy(
            src_ref=seen.at[core, tier, near, mem],
            dst_ref=seen.at[core, tier, near, mem],
            send_sem=obs_send.at[0],
            recv_sem=obs_recv.at[0],
            device_id={"mem": lax.rem(mem + step, GROUP)},
            device_id_type=MESH,
        ).start()
        return 0

    lax.fori_loop(1, GROUP, tell, 0)

    ship(0, SHARES[0], False)
    for part in range(STRIP):
        arrived[part, mem] = field[:, STEPS + STRIP * mem + part]

    whole = seen.at[0, 0, 0, pl.ds(0, GROUP - 1)]
    pltpu.make_async_copy(whole, whole, obs_recv.at[0]).wait()

    def pass_on(block, other, number):
        copy = pltpu.make_async_remote_copy(
            src_ref=block,
            dst_ref=block,
            send_sem=obs_send.at[number],
            recv_sem=obs_recv.at[number],
            device_id={"sub": other},
            device_id_type=MESH,
        )
        copy.start()
        return copy

    own = seen.at[core, tier, near]
    met = seen.at[core, tier, 1 - near]
    crossing = pass_on(own, across, 1)
    for other in tiers:
        pass_on(own, other, 2)
    ship(SHARES[0], SHARES[1], False)
    crossing.wait_recv()
    for other in tiers:
        pass_on(met, other, 3)
    ship(SHARES[1], SHARES[2], False)
    third = seen.at[0, pl.ds(0, 3), 0]
    pltpu.make_async_copy(third, third, obs_recv.at[2]).wait()
    pltpu.make_async_copy(third, third, obs_recv.at[3]).wait()
    swap = pass_on(seen.at[core], twin, 4)
    ship(SHARES[2], SHARES[3], False)
    swap.wait_recv()
    ship(SHARES[3], STRIP * (GROUP - 1), False)

    blocks = taper_ref.shape[0]
    lines = blocks * ENS
    gram[...] = jnp.zeros_like(gram)

    def gather_gram(index, _):
        lefts, rights = [], []
        for close in range(2):
            place = lax.rem(index, 4)
            sheet = lax.div(index, 4)
            observed = seen[sheet, place, close].reshape(ENS, OBS_SUB)
            mean = jnp.mean(observed, axis=0, keepdims=True)
            pert = observed - mean
            at = pl.ds(pl.multiple_of((4 * place + 2 * close + sheet) * OBS_SUB, OBS_SUB), OBS_SUB)
            weight = taper_ref[:, at] * precision_ref[:, at]
            pulling = weight * (values_ref[:, at] - mean)
            stack = [pert * weight[b : b + 1] for b in range(blocks)]
            lefts.append(side(jnp.concatenate([*stack, pulling, jnp.zeros_like(pulling)], axis=0)))
            high, low = halves(pert)
            rights.append(
                jnp.concatenate(
                    [jnp.concatenate([high, high], axis=1), jnp.concatenate([low, low], axis=1)], axis=0
                )
            )
        gram[...] += lax.dot_general(
            jnp.concatenate(lefts, axis=1),
            jnp.concatenate(rights, axis=1),
            (((1,), (1,)), ((), ())),
            preferred_element_type=F32,
        )
        return 0

    lax.fori_loop(0, GROUP // 2, gather_gram, 0)

    diagonal = lax.broadcasted_iota(jnp.int32, (ENS, ENS), 0) == lax.broadcasted_iota(
        jnp.int32, (ENS, ENS), 1
    )
    eye = jnp.where(diagonal, 1.0, 0.0)
    scales = []
    for b in range(blocks):
        wide = gram[b * ENS : (b + 1) * ENS, :]
        full = wide[:, :ENS] + wide[:, ENS:] + (ENS - 1.0) * eye
        scale = jnp.sum(jnp.sum(full * eye, axis=1, keepdims=True), axis=0, keepdims=True)
        scales.append(scale)
        start = full / scale
        factor = 1.5 * eye - 0.5 * start
        iterate[b] = product(side(start), tile(factor))
        root[b] = factor

    def sweep(_, carry):
        for b in range(blocks):
            held, base = iterate[b], root[b]
            factor = 1.5 * eye - 0.5 * product(side(base), tile(held))
            iterate[b] = product(side(held), tile(factor))
            root[b] = product(side(factor), tile(base))
        return carry

    lax.fori_loop(1, NS_ITERS - 1, sweep, 0)

    for b in range(blocks):
        factor = 1.5 * eye - 0.5 * product(side(root[b]), tile(iterate[b]))
        final = product(side(factor), tile(root[b])) / jnp.sqrt(scales[b])
        wide = gram[lines : lines + 8, :]
        pulled = (wide[:, :ENS] + wide[:, ENS:])[b : b + 1]
        pulled = jnp.broadcast_to(pulled, (16, ENS))
        right = tile(final)
        shift = product(side(product(side(pulled), right)), right)
        iterate[b] = math.sqrt(ENS - 1.0) * final + shift[0:1]

    def keep_own(part):
        return pltpu.make_async_copy(
            leaving.at[part, mem], settled.at[:, STRIP * mem + part], keep_sem.at[part]
        )

    def settle(part):
        for half in range(COLS // BLOCK):
            mixing = side(iterate[2 * part + half])
            cut = slice(half * BLOCK, (half + 1) * BLOCK)
            x = jnp.concatenate(
                [arrived[part, :, index, :, cut].reshape(ENS, BLOCK) for index in range(2)], axis=1
            )
            center = jnp.mean(x, axis=0, keepdims=True)
            moved = product(mixing, tile(x - center)) + center
            for index in range(2):
                leaving[part, :, index, :, cut] = moved[:, index * BLOCK : (index + 1) * BLOCK].reshape(
                    GROUP, OWN, BLOCK
                )

        def back(step, _):
            peer = lax.rem(mem + step, GROUP)
            pltpu.make_async_remote_copy(
                src_ref=leaving.at[part, peer],
                dst_ref=settled.at[:, STRIP * mem + part],
                send_sem=back_send,
                recv_sem=back_recv,
                device_id={"mem": peer},
                device_id_type=MESH,
            ).start()
            return 0

        lax.fori_loop(1, GROUP, back, 0)
        keep_own(part).start()

    for part in range(STRIP):
        strip = arrived.at[0, pl.ds(0, GROUP - 1)]
        pltpu.make_async_copy(strip, strip, out_recv.at[part]).wait()
        settle(part)

    everything = arrived.at[:, pl.ds(0, GROUP - 1)]
    pltpu.make_async_copy(everything, everything, back_recv).wait()

    for part in range(STRIP):
        keep_own(part).wait()
    for copy in rims:
        copy.wait_send()
    pltpu.make_async_copy(whole, whole, obs_send.at[0]).wait()
    pltpu.make_async_copy(own, own, obs_send.at[1]).wait()
    pltpu.make_async_copy(third, third, obs_send.at[2]).wait()
    pltpu.make_async_copy(third, third, obs_send.at[3]).wait()
    pltpu.make_async_copy(seen.at[0], seen.at[0], obs_send.at[4]).wait()
    pltpu.make_async_copy(everything, everything, out_send).wait()
    pltpu.make_async_copy(everything, everything, back_send).wait()


def turn_back(settled_hbm, now_hbm, prev_hbm, rows, turned, load_sem, store_sem):
    places = [(index, slice(at, at + CHUNK)) for index in range(2) for at in range(0, ROWS, CHUNK)]

    def load(number):
        index, at = places[number]
        return pltpu.make_async_copy(settled_hbm.at[index, at], rows.at[index, at], load_sem.at[number])

    def store(number):
        index, at = places[number]
        out = (now_hbm, prev_hbm)[index]
        return pltpu.make_async_copy(turned.at[index, :, at], out.at[:, at], store_sem.at[number])

    for number in range(len(places)):
        load(number).start()
    for number, (index, at) in enumerate(places):
        load(number).wait()
        turned[index, :, at] = jnp.transpose(rows[index, at], (1, 0, 2))
        store(number).start()
    for number in range(len(places)):
        store(number).wait()


def local(now_field, prev_field, speed, obs_cells, obs_values, obs_precision, taper):
    blocks = taper.shape[0]
    hbm = pl.BlockSpec(memory_space=pltpu.HBM)
    vmem = pl.BlockSpec(memory_space=pltpu.VMEM)
    outs = jax.ShapeDtypeStruct((OWN, ROWS, COLS), F32)
    settled = pl.pallas_call(
        kernel,
        out_shape=jax.ShapeDtypeStruct((2, ROWS, OWN, COLS), F32),
        in_specs=[hbm, hbm, hbm, pl.BlockSpec(memory_space=pltpu.SMEM), vmem, vmem, vmem],
        out_specs=hbm,
        scratch_shapes=[
            pltpu.VMEM((2, OWN, ROWS, COLS), F32),
            pltpu.VMEM((2, 2, OWN, STEPS, COLS), F32),
            pltpu.VMEM((ROWS, COLS), F32),
            pltpu.VMEM((2, STEPS, COLS), F32),
            pltpu.VMEM((TALL, OWN, COLS), F32),
            pltpu.VMEM((2, TALL, OWN, COLS), F32),
            pltpu.VMEM((2, 4, 2, GROUP, OWN, OBS_SUB), F32),
            pltpu.VMEM((blocks * ENS + 16, 2 * ENS), F32),
            pltpu.VMEM((blocks, ENS, ENS), F32),
            pltpu.VMEM((blocks, ENS, ENS), F32),
            pltpu.VMEM((STRIP, GROUP, 2, OWN, COLS), F32),
            pltpu.VMEM((STRIP, GROUP, 2, OWN, COLS), F32),
            pltpu.SemaphoreType.DMA((3,)),
            pltpu.SemaphoreType.DMA((2, 3)),
            pltpu.SemaphoreType.DMA((2, 3)),
            pltpu.SemaphoreType.DMA((5,)),
            pltpu.SemaphoreType.DMA((5,)),
            pltpu.SemaphoreType.DMA,
            pltpu.SemaphoreType.DMA((STRIP,)),
            pltpu.SemaphoreType.DMA,
            pltpu.SemaphoreType.DMA,
            pltpu.SemaphoreType.DMA((STRIP,)),
        ],
        compiler_params=pltpu.CompilerParams(
            collective_id=0, has_side_effects=True, vmem_limit_bytes=60 * 2**20
        ),
    )(
        now_field,
        prev_field,
        speed,
        obs_cells,
        obs_values[None, :],
        obs_precision[None, :],
        taper,
    )
    copies = 2 * ROWS // CHUNK
    return pl.pallas_call(
        turn_back,
        out_shape=(outs, outs),
        in_specs=[hbm],
        out_specs=(hbm, hbm),
        scratch_shapes=[
            pltpu.VMEM((2, ROWS, OWN, COLS), F32),
            pltpu.VMEM((2, OWN, ROWS, COLS), F32),
            pltpu.SemaphoreType.DMA((copies,)),
            pltpu.SemaphoreType.DMA((copies,)),
        ],
        compiler_params=pltpu.CompilerParams(vmem_limit_bytes=60 * 2**20),
    )(settled)


def solution(mesh):
    placed = (
        P("mem", "sub", None),
        P("mem", "sub", None),
        P("sub", None),
        P("sub"),
        P(),
        P(),
        P(("sub", "mem"), None),
    )
    return jax.shard_map(
        local,
        mesh=mesh,
        in_specs=placed,
        out_specs=(P("mem", "sub", None), P("mem", "sub", None)),
        check_vma=False,
    )
```

```python
import functools
import math

import jax
import jax.numpy as jnp
from jax import lax
from jax.experimental import pallas as pl
from jax.experimental.pallas import tpu as pltpu
from jax.sharding import PartitionSpec as P

ENS = 128
STEPS = 8
NS_ITERS = 8
BLOCK = 256
GROUP = 16
OWN = 8
ROWS = 64
STRIP = 4
COLS = 512
CHUNK = 16
OBS_SUB = 128
TALL = ROWS + 2 * STEPS
AHEAD = -1
MARGIN = 4
SHY = (STEPS + MARGIN) // STRIP
EARLY = 1
FIRST = 15
SHARES = (15, 24, 34, 44)
MESH = pl.DeviceIdType.MESH
F32 = jnp.float32


def halves(x):
    high = x.astype(jnp.bfloat16)
    low = (x - high.astype(F32)).astype(jnp.bfloat16)
    return high, low


def side(x):
    return jnp.concatenate(halves(x), axis=1)


def tile(x):
    both = side(x)
    return jnp.concatenate([both, both], axis=0)


def product(left, right):
    wide = jnp.dot(left, right, preferred_element_type=F32)
    width = wide.shape[1] // 2
    return wide[:, :width] + wide[:, width:]


def forecast_rows(field, pace, keep, step, low, high):
    source, target = (step + 1) % 2, step % 2
    lane = lax.broadcasted_iota(jnp.int32, (high - low, OWN, COLS), 2)
    here = field[source, low:high]
    west = jnp.where(lane == 0, 0.0, pltpu.roll(here, 1, 2))
    east = jnp.where(lane == COLS - 1, 0.0, pltpu.roll(here, COLS - 1, 2))
    beside = field[source, low + 1 : high + 1] + field[source, low - 1 : high - 1] + east + west
    return keep[low:high] * here - field[target, low:high] + pace[low:high] * beside


def kernel(
    now_hbm,
    prev_hbm,
    speed_hbm,
    cells_ref,
    values_ref,
    precision_ref,
    taper_ref,
    settled,
    raw,
    rim,
    pace_raw,
    pace_rim,
    pace,
    hold,
    field,
    seen,
    gram,
    iterate,
    root,
    arrived,
    leaving,
    load_sem,
    rim_send,
    rim_recv,
    obs_send,
    obs_recv,
    out_send,
    out_recv,
    back_send,
    back_recv,
    keep_sem,
):
    mem, sub = lax.axis_index("mem"), lax.axis_index("sub")
    core = lax.rem(sub, 2)
    near = lax.rem(lax.div(sub, 2), 2)
    tier = lax.div(sub, 4)
    above = lax.rem(sub + GROUP - 1, GROUP)
    below = lax.rem(sub + 1, GROUP)
    twin = sub + 1 - 2 * core
    across = sub + 2 - 4 * near
    tiers = [lax.rem(sub + 4 * k, GROUP) for k in (1, 2, 3)]

    barrier = pltpu.get_barrier_semaphore()
    for other in (above, below, twin, across, *tiers):
        pl.semaphore_signal(barrier, inc=1, device_id={"sub": other}, device_id_type=MESH)

    def greet(step, _):
        pl.semaphore_signal(
            barrier, inc=1, device_id={"mem": lax.rem(mem + step, GROUP)}, device_id_type=MESH
        )
        return 0

    lax.fori_loop(1, GROUP, greet, 0)

    def meet():
        pl.semaphore_wait(barrier, GROUP - 1 + 7)

        rims = []
        for side_index, (other, first) in enumerate(((below, ROWS - STEPS), (above, 0))):
            for index, source in enumerate((now_hbm, prev_hbm)):
                rims.append(
                    pltpu.make_async_remote_copy(
                        src_ref=source.at[:, first : first + STEPS, :],
                        dst_ref=rim.at[side_index, index],
                        send_sem=rim_send.at[side_index, index],
                        recv_sem=rim_recv.at[side_index, index],
                        device_id={"sub": other},
                        device_id_type=MESH,
                    )
                )
            rims.append(
                pltpu.make_async_remote_copy(
                    src_ref=speed_hbm.at[first : first + STEPS, :],
                    dst_ref=pace_rim.at[side_index],
                    send_sem=rim_send.at[side_index, 2],
                    recv_sem=rim_recv.at[side_index, 2],
                    device_id={"sub": other},
                    device_id_type=MESH,
                )
            )
        for copy in rims:
            copy.start()
        return rims

    loads = [
        pltpu.make_async_copy(now_hbm, raw.at[0], load_sem.at[0]),
        pltpu.make_async_copy(prev_hbm, raw.at[1], load_sem.at[1]),
        pltpu.make_async_copy(speed_hbm, pace_raw, load_sem.at[2]),
    ]
    for load in loads:
        load.start()
    if AHEAD < 0:
        rims = meet()
    for load in loads:
        load.wait()

    def turn(group, _):
        at = pl.multiple_of(group * 8, 8)
        for index in range(2):
            field[index, pl.ds(at + STEPS, 8)] = jnp.transpose(raw[index, :, pl.ds(at, 8), :], (1, 0, 2))
        rows = pace_raw[pl.ds(at, 8), :]
        pace[pl.ds(at + STEPS, 8)] = jnp.broadcast_to(rows[:, None, :], (8, OWN, COLS))
        hold[pl.ds(at + STEPS, 8)] = jnp.broadcast_to((2.0 - 4.0 * rows)[:, None, :], (8, OWN, COLS))
        return 0

    lax.fori_loop(0, ROWS // 8, turn, 0)

    def inner(step):
        low, high = STEPS + MARGIN + step, STEPS + ROWS - MARGIN - step
        field[step % 2, low:high] = forecast_rows(field, pace, hold, step, low, high)

    for step in range(1, AHEAD + 1):
        inner(step)

    if AHEAD >= 0:
        rims = meet()
    for step in range(max(AHEAD, 0) + 1, STEPS + 1):
        inner(step)


    def ship(first, last, early):
        def one(number, _):
            part = lax.div(number, GROUP - 1)
            step = lax.rem(number, GROUP - 1) + 1
            peer = lax.rem(mem + step, GROUP)
            ahead = jnp.logical_and(
                jnp.logical_and(peer >= SHY, peer < GROUP - SHY), jnp.logical_and(part < EARLY, step <= FIRST)
            )

            @pl.when(ahead if early else jnp.logical_not(ahead))
            def _():
                pltpu.make_async_remote_copy(
                    src_ref=field.at[:, STEPS + STRIP * peer + part],
                    dst_ref=arrived.at[part, mem],
                    send_sem=out_send,
                    recv_sem=out_recv.at[part],
                    device_id={"mem": peer},
                    device_id_type=MESH,
                ).start()

            return 0

        lax.fori_loop(first, last, one, 0)

    if FIRST:
        ship(0, EARLY * (GROUP - 1), True)

    for copy in rims:
        copy.wait_recv()
    for side_index, (at, outside) in enumerate(((0, sub == 0), (STEPS + ROWS, sub == GROUP - 1))):
        keep = jnp.where(outside, 0.0, 1.0)
        for index in range(2):
            field[index, at : at + STEPS] = jnp.transpose(rim[side_index, index], (1, 0, 2)) * keep
        rows = pace_rim[side_index] * keep
        pace[at : at + STEPS] = jnp.broadcast_to(rows[:, None, :], (STEPS, OWN, COLS))
        hold[at : at + STEPS] = jnp.broadcast_to((2.0 - 4.0 * rows)[:, None, :], (STEPS, OWN, COLS))
    for step in range(1, STEPS + 1):
        tops = step, STEPS + MARGIN + step
        ends = STEPS + ROWS - MARGIN - step, TALL - step
        upper = forecast_rows(field, pace, hold, step, *tops)
        lower = forecast_rows(field, pace, hold, step, *ends)
        field[step % 2, tops[0] : tops[1]] = upper
        field[step % 2, ends[0] : ends[1]] = lower

    lane_all = lax.broadcasted_iota(jnp.int32, (OWN, COLS), 1)
    lane = lax.broadcasted_iota(jnp.int32, (OWN, OBS_SUB), 1)

    def pick(index, held):
        cell = cells_ref[index]
        row = field[0, STEPS + lax.div(cell, COLS)]
        kept = jnp.where(lane_all == lax.rem(cell, COLS), row, 0.0)
        kept = kept[:, :128] + kept[:, 128:256] + kept[:, 256:384] + kept[:, 384:]
        return jnp.where(lane == index, jnp.sum(kept, axis=1, keepdims=True), held)

    seen[core, tier, near, mem] = lax.fori_loop(
        0, OBS_SUB, pick, jnp.zeros((OWN, OBS_SUB), F32), unroll=8
    )

    def tell(step, _):
        pltpu.make_async_remote_copy(
            src_ref=seen.at[core, tier, near, mem],
            dst_ref=seen.at[core, tier, near, mem],
            send_sem=obs_send.at[0],
            recv_sem=obs_recv.at[0],
            device_id={"mem": lax.rem(mem + step, GROUP)},
            device_id_type=MESH,
        ).start()
        return 0

    lax.fori_loop(1, GROUP, tell, 0)

    ship(0, SHARES[0], False)
    for part in range(STRIP):
        arrived[part, mem] = field[:, STEPS + STRIP * mem + part]

    whole = seen.at[0, 0, 0, pl.ds(0, GROUP - 1)]
    pltpu.make_async_copy(whole, whole, obs_recv.at[0]).wait()

    def pass_on(block, other, number):
        copy = pltpu.make_async_remote_copy(
            src_ref=block,
            dst_ref=block,
            send_sem=obs_send.at[number],
            recv_sem=obs_recv.at[number],
            device_id={"sub": other},
            device_id_type=MESH,
        )
        copy.start()
        return copy

    own = seen.at[core, tier, near]
    met = seen.at[core, tier, 1 - near]
    crossing = pass_on(own, across, 1)
    for other in tiers:
        pass_on(own, other, 2)
    ship(SHARES[0], SHARES[1], False)
    crossing.wait_recv()
    for other in tiers:
        pass_on(met, other, 3)
    ship(SHARES[1], SHARES[2], False)
    third = seen.at[0, pl.ds(0, 3), 0]
    pltpu.make_async_copy(third, third, obs_recv.at[2]).wait()
    pltpu.make_async_copy(third, third, obs_recv.at[3]).wait()
    swap = pass_on(seen.at[core], twin, 4)
    ship(SHARES[2], SHARES[3], False)
    swap.wait_recv()
    ship(SHARES[3], STRIP * (GROUP - 1), False)

    blocks = taper_ref.shape[0]
    lines = blocks * ENS
    gram[...] = jnp.zeros_like(gram)

    def gather_gram(index, _):
        lefts, rights = [], []
        for close in range(2):
            place = lax.rem(index, 4)
            sheet = lax.div(index, 4)
            observed = seen[sheet, place, close].reshape(ENS, OBS_SUB)
            mean = jnp.mean(observed, axis=0, keepdims=True)
            pert = observed - mean
            at = pl.ds(pl.multiple_of((4 * place + 2 * close + sheet) * OBS_SUB, OBS_SUB), OBS_SUB)
            weight = taper_ref[:, at] * precision_ref[:, at]
            pulling = weight * (values_ref[:, at] - mean)
            stack = [pert * weight[b : b + 1] for b in range(blocks)]
            lefts.append(side(jnp.concatenate([*stack, pulling, jnp.zeros_like(pulling)], axis=0)))
            high, low = halves(pert)
            rights.append(
                jnp.concatenate(
                    [jnp.concatenate([high, high], axis=1), jnp.concatenate([low, low], axis=1)], axis=0
                )
            )
        gram[...] += lax.dot_general(
            jnp.concatenate(lefts, axis=1),
            jnp.concatenate(rights, axis=1),
            (((1,), (1,)), ((), ())),
            preferred_element_type=F32,
        )
        return 0

    lax.fori_loop(0, GROUP // 2, gather_gram, 0)

    diagonal = lax.broadcasted_iota(jnp.int32, (ENS, ENS), 0) == lax.broadcasted_iota(
        jnp.int32, (ENS, ENS), 1
    )
    eye = jnp.where(diagonal, 1.0, 0.0)
    scales = []
    for b in range(blocks):
        wide = gram[b * ENS : (b + 1) * ENS, :]
        full = wide[:, :ENS] + wide[:, ENS:] + (ENS - 1.0) * eye
        scale = jnp.sum(jnp.sum(full * eye, axis=1, keepdims=True), axis=0, keepdims=True)
        scales.append(scale)
        start = full / scale
        factor = 1.5 * eye - 0.5 * start
        iterate[b] = product(side(start), tile(factor))
        root[b] = factor

    def sweep(_, carry):
        for b in range(blocks):
            held, base = iterate[b], root[b]
            factor = 1.5 * eye - 0.5 * product(side(base), tile(held))
            iterate[b] = product(side(held), tile(factor))
            root[b] = product(side(factor), tile(base))
        return carry

    lax.fori_loop(1, NS_ITERS - 1, sweep, 0)

    for b in range(blocks):
        factor = 1.5 * eye - 0.5 * product(side(root[b]), tile(iterate[b]))
        final = product(side(factor), tile(root[b])) / jnp.sqrt(scales[b])
        wide = gram[lines : lines + 8, :]
        pulled = (wide[:, :ENS] + wide[:, ENS:])[b : b + 1]
        pulled = jnp.broadcast_to(pulled, (16, ENS))
        right = tile(final)
        shift = product(side(product(side(pulled), right)), right)
        iterate[b] = math.sqrt(ENS - 1.0) * final + shift[0:1]

    def keep_own(part):
        return pltpu.make_async_copy(
            leaving.at[part, mem], settled.at[:, STRIP * mem + part], keep_sem.at[part]
        )

    def settle(part):
        for half in range(COLS // BLOCK):
            mixing = side(iterate[2 * part + half])
            cut = slice(half * BLOCK, (half + 1) * BLOCK)
            x = jnp.concatenate(
                [arrived[part, :, index, :, cut].reshape(ENS, BLOCK) for index in range(2)], axis=1
            )
            center = jnp.mean(x, axis=0, keepdims=True)
            moved = product(mixing, tile(x - center)) + center
            for index in range(2):
                leaving[part, :, index, :, cut] = moved[:, index * BLOCK : (index + 1) * BLOCK].reshape(
                    GROUP, OWN, BLOCK
                )

        def back(step, _):
            peer = lax.rem(mem + step, GROUP)
            pltpu.make_async_remote_copy(
                src_ref=leaving.at[part, peer],
                dst_ref=settled.at[:, STRIP * mem + part],
                send_sem=back_send,
                recv_sem=back_recv,
                device_id={"mem": peer},
                device_id_type=MESH,
            ).start()
            return 0

        lax.fori_loop(1, GROUP, back, 0)
        keep_own(part).start()

    for part in range(STRIP):
        strip = arrived.at[0, pl.ds(0, GROUP - 1)]
        pltpu.make_async_copy(strip, strip, out_recv.at[part]).wait()
        settle(part)

    everything = arrived.at[:, pl.ds(0, GROUP - 1)]
    pltpu.make_async_copy(everything, everything, back_recv).wait()

    for part in range(STRIP):
        keep_own(part).wait()
    for copy in rims:
        copy.wait_send()
    pltpu.make_async_copy(whole, whole, obs_send.at[0]).wait()
    pltpu.make_async_copy(own, own, obs_send.at[1]).wait()
    pltpu.make_async_copy(third, third, obs_send.at[2]).wait()
    pltpu.make_async_copy(third, third, obs_send.at[3]).wait()
    pltpu.make_async_copy(seen.at[0], seen.at[0], obs_send.at[4]).wait()
    pltpu.make_async_copy(everything, everything, out_send).wait()
    pltpu.make_async_copy(everything, everything, back_send).wait()


def turn_back(settled_hbm, now_hbm, prev_hbm, rows, turned, load_sem, store_sem):
    places = [(index, slice(at, at + CHUNK)) for index in range(2) for at in range(0, ROWS, CHUNK)]

    def load(number):
        index, at = places[number]
        return pltpu.make_async_copy(settled_hbm.at[index, at], rows.at[index, at], load_sem.at[number])

    def store(number):
        index, at = places[number]
        out = (now_hbm, prev_hbm)[index]
        return pltpu.make_async_copy(turned.at[index, :, at], out.at[:, at], store_sem.at[number])

    for number in range(len(places)):
        load(number).start()
    for number, (index, at) in enumerate(places):
        load(number).wait()
        turned[index, :, at] = jnp.transpose(rows[index, at], (1, 0, 2))
        store(number).start()
    for number in range(len(places)):
        store(number).wait()


def local(now_field, prev_field, speed, obs_cells, obs_values, obs_precision, taper):
    blocks = taper.shape[0]
    hbm = pl.BlockSpec(memory_space=pltpu.HBM)
    vmem = pl.BlockSpec(memory_space=pltpu.VMEM)
    outs = jax.ShapeDtypeStruct((OWN, ROWS, COLS), F32)
    settled = pl.pallas_call(
        kernel,
        out_shape=jax.ShapeDtypeStruct((2, ROWS, OWN, COLS), F32),
        in_specs=[hbm, hbm, hbm, pl.BlockSpec(memory_space=pltpu.SMEM), vmem, vmem, vmem],
        out_specs=hbm,
        scratch_shapes=[
            pltpu.VMEM((2, OWN, ROWS, COLS), F32),
            pltpu.VMEM((2, 2, OWN, STEPS, COLS), F32),
            pltpu.VMEM((ROWS, COLS), F32),
            pltpu.VMEM((2, STEPS, COLS), F32),
            pltpu.VMEM((TALL, OWN, COLS), F32),
            pltpu.VMEM((TALL, OWN, COLS), F32),
            pltpu.VMEM((2, TALL, OWN, COLS), F32),
            pltpu.VMEM((2, 4, 2, GROUP, OWN, OBS_SUB), F32),
            pltpu.VMEM((blocks * ENS + 16, 2 * ENS), F32),
            pltpu.VMEM((blocks, ENS, ENS), F32),
            pltpu.VMEM((blocks, ENS, ENS), F32),
            pltpu.VMEM((STRIP, GROUP, 2, OWN, COLS), F32),
            pltpu.VMEM((STRIP, GROUP, 2, OWN, COLS), F32),
            pltpu.SemaphoreType.DMA((3,)),
            pltpu.SemaphoreType.DMA((2, 3)),
            pltpu.SemaphoreType.DMA((2, 3)),
            pltpu.SemaphoreType.DMA((5,)),
            pltpu.SemaphoreType.DMA((5,)),
            pltpu.SemaphoreType.DMA,
            pltpu.SemaphoreType.DMA((STRIP,)),
            pltpu.SemaphoreType.DMA,
            pltpu.SemaphoreType.DMA,
            pltpu.SemaphoreType.DMA((STRIP,)),
        ],
        compiler_params=pltpu.CompilerParams(
            collective_id=0, has_side_effects=True, vmem_limit_bytes=60 * 2**20
        ),
    )(
        now_field,
        prev_field,
        speed,
        obs_cells,
        obs_values[None, :],
        obs_precision[None, :],
        taper,
    )
    copies = 2 * ROWS // CHUNK
    return pl.pallas_call(
        turn_back,
        out_shape=(outs, outs),
        in_specs=[hbm],
        out_specs=(hbm, hbm),
        scratch_shapes=[
            pltpu.VMEM((2, ROWS, OWN, COLS), F32),
            pltpu.VMEM((2, OWN, ROWS, COLS), F32),
            pltpu.SemaphoreType.DMA((copies,)),
            pltpu.SemaphoreType.DMA((copies,)),
        ],
        compiler_params=pltpu.CompilerParams(vmem_limit_bytes=60 * 2**20),
    )(settled)


def solution(mesh):
    placed = (
        P("mem", "sub", None),
        P("mem", "sub", None),
        P("sub", None),
        P("sub"),
        P(),
        P(),
        P(("sub", "mem"), None),
    )
    return jax.shard_map(
        local,
        mesh=mesh,
        in_specs=placed,
        out_specs=(P("mem", "sub", None), P("mem", "sub", None)),
        check_vma=False,
    )
```

```python
import functools
import math

import jax
import jax.numpy as jnp
from jax import lax
from jax.experimental import pallas as pl
from jax.experimental.pallas import tpu as pltpu
from jax.sharding import PartitionSpec as P

ENS = 128
STEPS = 8
NS_ITERS = 8
BLOCK = 256
GROUP = 16
OWN = 8
ROWS = 64
STRIP = 4
COLS = 512
CHUNK = 16
OBS_SUB = 128
TALL = ROWS + 2 * STEPS
AHEAD = -1
MARGIN = 4
SHY = (STEPS + MARGIN) // STRIP
EARLY = 1
FIRST = 15
SHARES = (18, 28, 40, 50)
MESH = pl.DeviceIdType.MESH
F32 = jnp.float32


def halves(x):
    high = x.astype(jnp.bfloat16)
    low = (x - high.astype(F32)).astype(jnp.bfloat16)
    return high, low


def side(x):
    return jnp.concatenate(halves(x), axis=1)


def tile(x):
    both = side(x)
    return jnp.concatenate([both, both], axis=0)


def product(left, right):
    wide = jnp.dot(left, right, preferred_element_type=F32)
    width = wide.shape[1] // 2
    return wide[:, :width] + wide[:, width:]


def forecast_rows(field, pace, keep, step, low, high):
    source, target = (step + 1) % 2, step % 2
    lane = lax.broadcasted_iota(jnp.int32, (high - low, OWN, COLS), 2)
    here = field[source, low:high]
    west = jnp.where(lane == 0, 0.0, pltpu.roll(here, 1, 2))
    east = jnp.where(lane == COLS - 1, 0.0, pltpu.roll(here, COLS - 1, 2))
    beside = field[source, low + 1 : high + 1] + field[source, low - 1 : high - 1] + east + west
    return keep[low:high] * here - field[target, low:high] + pace[low:high] * beside


def kernel(
    now_hbm,
    prev_hbm,
    speed_hbm,
    cells_ref,
    values_ref,
    precision_ref,
    taper_ref,
    settled,
    raw,
    rim,
    pace_raw,
    pace_rim,
    pace,
    hold,
    field,
    seen,
    gram,
    iterate,
    root,
    arrived,
    leaving,
    load_sem,
    rim_send,
    rim_recv,
    obs_send,
    obs_recv,
    out_send,
    out_recv,
    back_send,
    back_recv,
    keep_sem,
):
    mem, sub = lax.axis_index("mem"), lax.axis_index("sub")
    core = lax.rem(sub, 2)
    near = lax.rem(lax.div(sub, 2), 2)
    tier = lax.div(sub, 4)
    above = lax.rem(sub + GROUP - 1, GROUP)
    below = lax.rem(sub + 1, GROUP)
    twin = sub + 1 - 2 * core
    across = sub + 2 - 4 * near
    tiers = [lax.rem(sub + 4 * k, GROUP) for k in (1, 2, 3)]

    barrier = pltpu.get_barrier_semaphore()
    for other in (above, below, twin, across, *tiers):
        pl.semaphore_signal(barrier, inc=1, device_id={"sub": other}, device_id_type=MESH)

    def greet(step, _):
        pl.semaphore_signal(
            barrier, inc=1, device_id={"mem": lax.rem(mem + step, GROUP)}, device_id_type=MESH
        )
        return 0

    lax.fori_loop(1, GROUP, greet, 0)

    def meet():
        pl.semaphore_wait(barrier, GROUP - 1 + 7)

        rims = []
        for side_index, (other, first) in enumerate(((below, ROWS - STEPS), (above, 0))):
            for index, source in enumerate((now_hbm, prev_hbm)):
                rims.append(
                    pltpu.make_async_remote_copy(
                        src_ref=source.at[:, first : first + STEPS, :],
                        dst_ref=rim.at[side_index, index],
                        send_sem=rim_send.at[side_index, index],
                        recv_sem=rim_recv.at[side_index, index],
                        device_id={"sub": other},
                        device_id_type=MESH,
                    )
                )
            rims.append(
                pltpu.make_async_remote_copy(
                    src_ref=speed_hbm.at[first : first + STEPS, :],
                    dst_ref=pace_rim.at[side_index],
                    send_sem=rim_send.at[side_index, 2],
                    recv_sem=rim_recv.at[side_index, 2],
                    device_id={"sub": other},
                    device_id_type=MESH,
                )
            )
        for copy in rims:
            copy.start()
        return rims

    loads = [
        pltpu.make_async_copy(now_hbm, raw.at[0], load_sem.at[0]),
        pltpu.make_async_copy(prev_hbm, raw.at[1], load_sem.at[1]),
        pltpu.make_async_copy(speed_hbm, pace_raw, load_sem.at[2]),
    ]
    for load in loads:
        load.start()
    if AHEAD < 0:
        rims = meet()
    for load in loads:
        load.wait()

    def turn(group, _):
        at = pl.multiple_of(group * 8, 8)
        for index in range(2):
            field[index, pl.ds(at + STEPS, 8)] = jnp.transpose(raw[index, :, pl.ds(at, 8), :], (1, 0, 2))
        rows = pace_raw[pl.ds(at, 8), :]
        pace[pl.ds(at + STEPS, 8)] = jnp.broadcast_to(rows[:, None, :], (8, OWN, COLS))
        hold[pl.ds(at + STEPS, 8)] = jnp.broadcast_to((2.0 - 4.0 * rows)[:, None, :], (8, OWN, COLS))
        return 0

    lax.fori_loop(0, ROWS // 8, turn, 0)

    def inner(step):
        low, high = STEPS + MARGIN + step, STEPS + ROWS - MARGIN - step
        field[step % 2, low:high] = forecast_rows(field, pace, hold, step, low, high)

    for step in range(1, AHEAD + 1):
        inner(step)

    if AHEAD >= 0:
        rims = meet()
    for step in range(max(AHEAD, 0) + 1, STEPS + 1):
        inner(step)


    def ship(first, last, early):
        def one(number, _):
            part = lax.div(number, GROUP - 1)
            step = lax.rem(number, GROUP - 1) + 1
            peer = lax.rem(mem + step, GROUP)
            ahead = jnp.logical_and(
                jnp.logical_and(peer >= SHY, peer < GROUP - SHY), jnp.logical_and(part < EARLY, step <= FIRST)
            )

            @pl.when(ahead if early else jnp.logical_not(ahead))
            def _():
                pltpu.make_async_remote_copy(
                    src_ref=field.at[:, STEPS + STRIP * peer + part],
                    dst_ref=arrived.at[part, mem],
                    send_sem=out_send,
                    recv_sem=out_recv.at[part],
                    device_id={"mem": peer},
                    device_id_type=MESH,
                ).start()

            return 0

        lax.fori_loop(first, last, one, 0)

    if FIRST:
        ship(0, EARLY * (GROUP - 1), True)

    for copy in rims:
        copy.wait_recv()
    for side_index, (at, outside) in enumerate(((0, sub == 0), (STEPS + ROWS, sub == GROUP - 1))):
        keep = jnp.where(outside, 0.0, 1.0)
        for index in range(2):
            field[index, at : at + STEPS] = jnp.transpose(rim[side_index, index], (1, 0, 2)) * keep
        rows = pace_rim[side_index] * keep
        pace[at : at + STEPS] = jnp.broadcast_to(rows[:, None, :], (STEPS, OWN, COLS))
        hold[at : at + STEPS] = jnp.broadcast_to((2.0 - 4.0 * rows)[:, None, :], (STEPS, OWN, COLS))
    for step in range(1, STEPS + 1):
        tops = step, STEPS + MARGIN + step
        ends = STEPS + ROWS - MARGIN - step, TALL - step
        upper = forecast_rows(field, pace, hold, step, *tops)
        lower = forecast_rows(field, pace, hold, step, *ends)
        field[step % 2, tops[0] : tops[1]] = upper
        field[step % 2, ends[0] : ends[1]] = lower

    lane_all = lax.broadcasted_iota(jnp.int32, (OWN, COLS), 1)
    lane = lax.broadcasted_iota(jnp.int32, (OWN, OBS_SUB), 1)

    def pick(index, held):
        cell = cells_ref[index]
        row = field[0, STEPS + lax.div(cell, COLS)]
        kept = jnp.where(lane_all == lax.rem(cell, COLS), row, 0.0)
        kept = kept[:, :128] + kept[:, 128:256] + kept[:, 256:384] + kept[:, 384:]
        return jnp.where(lane == index, jnp.sum(kept, axis=1, keepdims=True), held)

    seen[core, tier, near, mem] = lax.fori_loop(
        0, OBS_SUB, pick, jnp.zeros((OWN, OBS_SUB), F32), unroll=8
    )

    def tell(step, _):
        pltpu.make_async_remote_copy(
            src_ref=seen.at[core, tier, near, mem],
            dst_ref=seen.at[core, tier, near, mem],
            send_sem=obs_send.at[0],
            recv_sem=obs_recv.at[0],
            device_id={"mem": lax.rem(mem + step, GROUP)},
            device_id_type=MESH,
        ).start()
        return 0

    lax.fori_loop(1, GROUP, tell, 0)

    ship(0, SHARES[0], False)
    for part in range(STRIP):
        arrived[part, mem] = field[:, STEPS + STRIP * mem + part]

    whole = seen.at[0, 0, 0, pl.ds(0, GROUP - 1)]
    pltpu.make_async_copy(whole, whole, obs_recv.at[0]).wait()

    def pass_on(block, other, number):
        copy = pltpu.make_async_remote_copy(
            src_ref=block,
            dst_ref=block,
            send_sem=obs_send.at[number],
            recv_sem=obs_recv.at[number],
            device_id={"sub": other},
            device_id_type=MESH,
        )
        copy.start()
        return copy

    own = seen.at[core, tier, near]
    met = seen.at[core, tier, 1 - near]
    crossing = pass_on(own, across, 1)
    for other in tiers:
        pass_on(own, other, 2)
    ship(SHARES[0], SHARES[1], False)
    crossing.wait_recv()
    for other in tiers:
        pass_on(met, other, 3)
    ship(SHARES[1], SHARES[2], False)
    third = seen.at[0, pl.ds(0, 3), 0]
    pltpu.make_async_copy(third, third, obs_recv.at[2]).wait()
    pltpu.make_async_copy(third, third, obs_recv.at[3]).wait()
    swap = pass_on(seen.at[core], twin, 4)
    ship(SHARES[2], SHARES[3], False)
    swap.wait_recv()
    ship(SHARES[3], STRIP * (GROUP - 1), False)

    blocks = taper_ref.shape[0]
    lines = blocks * ENS
    gram[...] = jnp.zeros_like(gram)

    def gather_gram(index, _):
        lefts, rights = [], []
        for close in range(2):
            place = lax.rem(index, 4)
            sheet = lax.div(index, 4)
            observed = seen[sheet, place, close].reshape(ENS, OBS_SUB)
            mean = jnp.mean(observed, axis=0, keepdims=True)
            pert = observed - mean
            at = pl.ds(pl.multiple_of((4 * place + 2 * close + sheet) * OBS_SUB, OBS_SUB), OBS_SUB)
            weight = taper_ref[:, at] * precision_ref[:, at]
            pulling = weight * (values_ref[:, at] - mean)
            stack = [pert * weight[b : b + 1] for b in range(blocks)]
            lefts.append(side(jnp.concatenate([*stack, pulling, jnp.zeros_like(pulling)], axis=0)))
            high, low = halves(pert)
            rights.append(
                jnp.concatenate(
                    [jnp.concatenate([high, high], axis=1), jnp.concatenate([low, low], axis=1)], axis=0
                )
            )
        gram[...] += lax.dot_general(
            jnp.concatenate(lefts, axis=1),
            jnp.concatenate(rights, axis=1),
            (((1,), (1,)), ((), ())),
            preferred_element_type=F32,
        )
        return 0

    lax.fori_loop(0, GROUP // 2, gather_gram, 0)

    diagonal = lax.broadcasted_iota(jnp.int32, (ENS, ENS), 0) == lax.broadcasted_iota(
        jnp.int32, (ENS, ENS), 1
    )
    eye = jnp.where(diagonal, 1.0, 0.0)
    scales = []
    for b in range(blocks):
        wide = gram[b * ENS : (b + 1) * ENS, :]
        full = wide[:, :ENS] + wide[:, ENS:] + (ENS - 1.0) * eye
        scale = jnp.sum(jnp.sum(full * eye, axis=1, keepdims=True), axis=0, keepdims=True)
        scales.append(scale)
        start = full / scale
        factor = 1.5 * eye - 0.5 * start
        iterate[b] = product(side(start), tile(factor))
        root[b] = factor

    def sweep(_, carry):
        for b in range(blocks):
            held, base = iterate[b], root[b]
            factor = 1.5 * eye - 0.5 * product(side(base), tile(held))
            iterate[b] = product(side(held), tile(factor))
            root[b] = product(side(factor), tile(base))
        return carry

    lax.fori_loop(1, NS_ITERS - 1, sweep, 0)

    for b in range(blocks):
        factor = 1.5 * eye - 0.5 * product(side(root[b]), tile(iterate[b]))
        final = product(side(factor), tile(root[b])) / jnp.sqrt(scales[b])
        wide = gram[lines : lines + 8, :]
        pulled = (wide[:, :ENS] + wide[:, ENS:])[b : b + 1]
        pulled = jnp.broadcast_to(pulled, (16, ENS))
        right = tile(final)
        shift = product(side(product(side(pulled), right)), right)
        iterate[b] = math.sqrt(ENS - 1.0) * final + shift[0:1]

    def keep_own(part):
        return pltpu.make_async_copy(
            leaving.at[part, mem], settled.at[:, STRIP * mem + part], keep_sem.at[part]
        )

    def settle(part):
        for half in range(COLS // BLOCK):
            mixing = side(iterate[2 * part + half])
            cut = slice(half * BLOCK, (half + 1) * BLOCK)
            x = jnp.concatenate(
                [arrived[part, :, index, :, cut].reshape(ENS, BLOCK) for index in range(2)], axis=1
            )
            center = jnp.mean(x, axis=0, keepdims=True)
            moved = product(mixing, tile(x - center)) + center
            for index in range(2):
                leaving[part, :, index, :, cut] = moved[:, index * BLOCK : (index + 1) * BLOCK].reshape(
                    GROUP, OWN, BLOCK
                )

        def back(step, _):
            peer = lax.rem(mem + step, GROUP)
            pltpu.make_async_remote_copy(
                src_ref=leaving.at[part, peer],
                dst_ref=settled.at[:, STRIP * mem + part],
                send_sem=back_send,
                recv_sem=back_recv,
                device_id={"mem": peer},
                device_id_type=MESH,
            ).start()
            return 0

        lax.fori_loop(1, GROUP, back, 0)
        keep_own(part).start()

    for part in range(STRIP):
        strip = arrived.at[0, pl.ds(0, GROUP - 1)]
        pltpu.make_async_copy(strip, strip, out_recv.at[part]).wait()
        settle(part)

    everything = arrived.at[:, pl.ds(0, GROUP - 1)]
    pltpu.make_async_copy(everything, everything, back_recv).wait()

    for part in range(STRIP):
        keep_own(part).wait()
    for copy in rims:
        copy.wait_send()
    pltpu.make_async_copy(whole, whole, obs_send.at[0]).wait()
    pltpu.make_async_copy(own, own, obs_send.at[1]).wait()
    pltpu.make_async_copy(third, third, obs_send.at[2]).wait()
    pltpu.make_async_copy(third, third, obs_send.at[3]).wait()
    pltpu.make_async_copy(seen.at[0], seen.at[0], obs_send.at[4]).wait()
    pltpu.make_async_copy(everything, everything, out_send).wait()
    pltpu.make_async_copy(everything, everything, back_send).wait()


def turn_back(settled_hbm, now_hbm, prev_hbm, rows, turned, load_sem, store_sem):
    places = [(index, slice(at, at + CHUNK)) for index in range(2) for at in range(0, ROWS, CHUNK)]

    def load(number):
        index, at = places[number]
        return pltpu.make_async_copy(settled_hbm.at[index, at], rows.at[index, at], load_sem.at[number])

    def store(number):
        index, at = places[number]
        out = (now_hbm, prev_hbm)[index]
        return pltpu.make_async_copy(turned.at[index, :, at], out.at[:, at], store_sem.at[number])

    for number in range(len(places)):
        load(number).start()
    for number, (index, at) in enumerate(places):
        load(number).wait()
        turned[index, :, at] = jnp.transpose(rows[index, at], (1, 0, 2))
        store(number).start()
    for number in range(len(places)):
        store(number).wait()


def local(now_field, prev_field, speed, obs_cells, obs_values, obs_precision, taper):
    blocks = taper.shape[0]
    hbm = pl.BlockSpec(memory_space=pltpu.HBM)
    vmem = pl.BlockSpec(memory_space=pltpu.VMEM)
    outs = jax.ShapeDtypeStruct((OWN, ROWS, COLS), F32)
    settled = pl.pallas_call(
        kernel,
        out_shape=jax.ShapeDtypeStruct((2, ROWS, OWN, COLS), F32),
        in_specs=[hbm, hbm, hbm, pl.BlockSpec(memory_space=pltpu.SMEM), vmem, vmem, vmem],
        out_specs=hbm,
        scratch_shapes=[
            pltpu.VMEM((2, OWN, ROWS, COLS), F32),
            pltpu.VMEM((2, 2, OWN, STEPS, COLS), F32),
            pltpu.VMEM((ROWS, COLS), F32),
            pltpu.VMEM((2, STEPS, COLS), F32),
            pltpu.VMEM((TALL, OWN, COLS), F32),
            pltpu.VMEM((TALL, OWN, COLS), F32),
            pltpu.VMEM((2, TALL, OWN, COLS), F32),
            pltpu.VMEM((2, 4, 2, GROUP, OWN, OBS_SUB), F32),
            pltpu.VMEM((blocks * ENS + 16, 2 * ENS), F32),
            pltpu.VMEM((blocks, ENS, ENS), F32),
            pltpu.VMEM((blocks, ENS, ENS), F32),
            pltpu.VMEM((STRIP, GROUP, 2, OWN, COLS), F32),
            pltpu.VMEM((STRIP, GROUP, 2, OWN, COLS), F32),
            pltpu.SemaphoreType.DMA((3,)),
            pltpu.SemaphoreType.DMA((2, 3)),
            pltpu.SemaphoreType.DMA((2, 3)),
            pltpu.SemaphoreType.DMA((5,)),
            pltpu.SemaphoreType.DMA((5,)),
            pltpu.SemaphoreType.DMA,
            pltpu.SemaphoreType.DMA((STRIP,)),
            pltpu.SemaphoreType.DMA,
            pltpu.SemaphoreType.DMA,
            pltpu.SemaphoreType.DMA((STRIP,)),
        ],
        compiler_params=pltpu.CompilerParams(
            collective_id=0, has_side_effects=True, vmem_limit_bytes=60 * 2**20
        ),
    )(
        now_field,
        prev_field,
        speed,
        obs_cells,
        obs_values[None, :],
        obs_precision[None, :],
        taper,
    )
    copies = 2 * ROWS // CHUNK
    return pl.pallas_call(
        turn_back,
        out_shape=(outs, outs),
        in_specs=[hbm],
        out_specs=(hbm, hbm),
        scratch_shapes=[
            pltpu.VMEM((2, ROWS, OWN, COLS), F32),
            pltpu.VMEM((2, OWN, ROWS, COLS), F32),
            pltpu.SemaphoreType.DMA((copies,)),
            pltpu.SemaphoreType.DMA((copies,)),
        ],
        compiler_params=pltpu.CompilerParams(vmem_limit_bytes=60 * 2**20),
    )(settled)


def solution(mesh):
    placed = (
        P("mem", "sub", None),
        P("mem", "sub", None),
        P("sub", None),
        P("sub"),
        P(),
        P(),
        P(("sub", "mem"), None),
    )
    return jax.shard_map(
        local,
        mesh=mesh,
        in_specs=placed,
        out_specs=(P("mem", "sub", None), P("mem", "sub", None)),
        check_vma=False,
    )
```
